256 devices in a mesh: req: 64 (over z, x, core), tp: 4 (over y).
Axes of the slice: x: 4, y: 4, z: 8, core: 2. Of those that a mesh axis runs over, the one named last changes fastest.
Arguments:
- patches: bfloat16 [65536, 1408], P('req')
- segment_ids: int32 [65536], P('req'), may hold values from 0 to 15, as said below
- grid_sides: int32 [65536], P('req'), may hold values from 8 to 32, as said below
- split_plan: int32 [64, 2], P('req'), may hold values from 0 to 960, as said below
- owner_dev: int32 [16384], P('req'), may hold values from 0 to 63, as said below
- dest_row: int32 [16384], P('req'), may hold values from 0 to 255, as said below
- ln_gain: float32 [1408], replicated, may hold values from 0.25 to 1.75
- ln_bias: float32 [1408], replicated, may hold values from -3 to 3
- w_qkv: bfloat16 [3, 1408, 1408], P(None, 'tp')
- w_out: bfloat16 [1408, 1408], P('tp'), may hold values from -0.625 to 0.625
- w_proj: bfloat16 [5632, 2048], P(None, 'tp'), may hold values from -0.078125 to 0.078125
Outputs:
- vision_tokens: bfloat16 [16384, 2048], P('req', 'tp')
The draws below stay inside these ranges and needn't reach their ends.
Inputs may be any that keep to these rules, and one draw needn't show every extreme that they name: `segment_ids`: within each packed row the ids start at 0, never fall, and one id's patches are contiguous; an image with grid side s has s * s patches (the last image of the whole packing may be cut short) and lies in at most two neighbouring rows. `grid_sides`: all patches of one image share its grid side, a multiple of 8. split_plan[r, 0] is the number of patches of row r's first image that lie in row r - 1, split_plan[r, 1] the number of patches of row r's last image that lie in row r + 1; both are 0 where no image crosses. `owner_dev`: the merged tokens of one row form blocks of 8 consecutive merged tokens; each block goes whole to one owner, a row's blocks go to different owners, and every owner receives 1024 // 4 merged tokens. `dest_row`: every row of every owner's output receives exactly one merged token.
All inputs are finite; a program needn't handle non-finite values.
Results may differ from the reference program's by a relative error of at most 0.019.
Values may be sent and summed in bfloat16 or wider, within the bound.
No kernel may reach another device: no remote copies, remote signals or barrier semaphores. Data moves between devices by JAX's collectives and lax.ppermute only.
A program may use at most 128 MiB of HBM per device.

```python
import math
import jax
import jax.numpy as jnp
from jax import lax

D = 1408
HEADS = 16
HD = 88
PROJ = 2048
SIDE_MIN = 8
SIDE_MAX = 32
TOK_DEV = 1024
TOKENS = 65536
MERGED = 16384
HEAD_GROUPS = 4
N_REQ = 64


def packing_layout(key):
    base_key = jax.random.fold_in(key, 4242)
    image_count = TOKENS // (SIDE_MIN * SIDE_MIN) + 1
    multiples = jax.random.randint(jax.random.fold_in(base_key, 1), (image_count,), 1, SIDE_MAX // SIDE_MIN + 1).astype(jnp.int32)
    halves = SIDE_MIN // 2 * multiples
    lead_count = TOK_DEV // (SIDE_MAX * SIDE_MAX)
    small_run = TOK_DEV // (SIDE_MIN * SIDE_MIN) - 1
    image_index = jnp.arange(image_count, dtype=jnp.int32)
    halves = jnp.where(image_index < lead_count - 1, SIDE_MAX // 2, halves)
    halves = jnp.where(image_index == lead_count - 1, SIDE_MIN // 2, halves)
    halves = jnp.where(image_index == lead_count, SIDE_MAX // 2, halves)
    halves = jnp.where((image_index > lead_count) & (image_index <= lead_count + small_run), SIDE_MIN // 2, halves).astype(jnp.int32)
    side_list = 2 * halves
    lengths = side_list * side_list
    end_at = jnp.cumsum(lengths).astype(jnp.int32)
    starts = end_at - lengths
    tok_index = jnp.arange(TOKENS, dtype=jnp.int32)
    image_id = jnp.searchsorted(end_at, tok_index, side='right').astype(jnp.int32)
    by_row = image_id.reshape(N_REQ, TOK_DEV)
    row_first = by_row[:, 0]
    row_last = by_row[:, TOK_DEV - 1]
    segment = (by_row - row_first[:, None]).reshape(TOKENS).astype(jnp.int32)
    token_side = side_list[image_id].astype(jnp.int32)
    row_begin = jnp.arange(N_REQ, dtype=jnp.int32) * TOK_DEV
    before = row_begin - starts[row_first]
    after_rows = jnp.maximum(end_at[row_last] - (row_begin + TOK_DEV), 0)
    after_rows = after_rows.at[N_REQ - 1].set(0)
    return (segment, token_side, jnp.stack([before, after_rows], axis=1).astype(jnp.int32))


def return_layout(key):
    base_key = jax.random.fold_in(key, 5151)
    merged_dev = TOK_DEV // 4
    block_count = N_REQ // 2
    block_size = TOK_DEV // (2 * N_REQ)
    offsets = jax.random.permutation(jax.random.fold_in(base_key, 1), N_REQ)[:block_count].astype(jnp.int32)
    merged_index = jnp.arange(MERGED, dtype=jnp.int32)
    device_id = merged_index // merged_dev
    local_index = merged_index % merged_dev
    block_id = local_index // block_size
    owner_id = (device_id + offsets[block_id]) % N_REQ
    slot_id = block_id * block_size + local_index % block_size
    ranked = jax.random.randint(jax.random.fold_in(base_key, 2), (N_REQ, merged_dev), 0, 1 << 20).astype(jnp.int32) * merged_dev + jnp.arange(merged_dev, dtype=jnp.int32)[None, :]
    shuffled = jnp.argsort(ranked, axis=1).astype(jnp.int32)
    return (owner_id.astype(jnp.int32), shuffled[owner_id, slot_id].astype(jnp.int32))


def draw_segment_ids(key, part):
    return packing_layout(key)[0]


def draw_grid_sides(key, part):
    return packing_layout(key)[1]


def draw_split_plan(key, part):
    return packing_layout(key)[2]


def draw_owner_dev(key, part):
    return return_layout(key)[0]


def draw_dest_row(key, part):
    return return_layout(key)[1]


def draw_patches(key, part):
    base_key, row_key, col_key = jax.random.split(key, 3)
    entries = jax.random.normal(base_key, (TOKENS, D), jnp.float32)
    row_scale = jnp.exp(jax.random.uniform(row_key, (TOKENS, 1), jnp.float32, math.log(0.3), math.log(3.0)))
    col_scale = jnp.exp(jax.random.uniform(col_key, (1, D), jnp.float32, math.log(0.3), math.log(3.0)))
    values = entries * row_scale * col_scale
    return values.astype(jnp.bfloat16)


def draw_w_qkv(key, part):
    entries = jax.random.normal(key, (3, D, D), jnp.float32) * D ** (-0.5)
    return entries.astype(jnp.bfloat16)


def steps_of(own_key, extent, shards, smallest, high):
    def one(dim, shards_of):
        draws = jax.random.uniform(jax.random.fold_in(jax.random.fold_in(own_key, 6), dim), (shards_of,), jnp.float32, smallest / len(shards), high / len(shards))
        return jnp.repeat(jnp.exp(draws), extent[dim] // shards_of).reshape((-1,) + (1,) * (len(extent) - dim - 1))

    level = one(*shards[0])
    for cut in shards[1:]:
        level = level * one(*cut)
    return level


def normal_values(stream_key, shape, width, reach, cuts=(), held_as=jnp.bfloat16):
    values = jax.random.normal(stream_key, shape, jnp.float32) * width
    if len(cuts) > 0:
        values = steps_of(stream_key, shape, cuts, -0.22, 0.18) * values
    return jnp.clip(values, min=-reach, max=reach).astype(held_as)


def setup_inputs(seed: int = 0) -> dict:
    keys = jax.random.split(jax.random.key(seed), 12)
    patches = draw_patches(jax.random.fold_in(keys[11], 71), 0)
    segment_ids = draw_segment_ids(jax.random.fold_in(keys[11], 71), 0)
    grid_sides = draw_grid_sides(jax.random.fold_in(keys[11], 71), 0)
    split_plan = draw_split_plan(jax.random.fold_in(keys[11], 71), 0)
    owner_dev = draw_owner_dev(jax.random.fold_in(keys[11], 71), 0)
    dest_row = draw_dest_row(jax.random.fold_in(keys[11], 71), 0)
    ln_gain = jnp.clip(1.0 + 0.15 * jax.random.normal(keys[6], (D,), jnp.float32), 0.25, 1.75)
    ln_bias = normal_values(keys[7], (D,), 0.5, 3.0, (), jnp.float32)
    w_qkv = draw_w_qkv(jax.random.fold_in(keys[11], 71), 0)
    w_out = normal_values(keys[9], (D, D), HD ** -0.5, 0.625, ((0, 4),))
    w_proj = normal_values(keys[10], (4 * D, PROJ), (4 * D) ** -0.5, 0.078125, ((1, 4),))
    return {"patches": patches, "segment_ids": segment_ids, "grid_sides": grid_sides, "split_plan": split_plan, "owner_dev": owner_dev, "dest_row": dest_row, "ln_gain": ln_gain, "ln_bias": ln_bias, "w_qkv": w_qkv, "w_out": w_out, "w_proj": w_proj}


def layer_norm(inputs, scale_vec, shift_vec):
    widened = inputs.astype(jnp.float32)
    centred = widened - lax.optimization_barrier(jnp.mean(widened, axis=-1, keepdims=True))
    variance = lax.optimization_barrier(jnp.mean(centred * centred, axis=-1, keepdims=True))
    return (centred * lax.rsqrt(variance + 1e-06) * scale_vec + shift_vec).astype(jnp.bfloat16)

def grid_positions(seg_row, side_row, first_offset):
    row_len = seg_row.shape[0]
    tok_index = jnp.arange(row_len, dtype=jnp.int32)
    boundary = jnp.concatenate([jnp.ones((1,), dtype=bool), seg_row[1:] != seg_row[:-1]])
    seg_start = lax.cummax(jnp.where(boundary, tok_index, 0).astype(jnp.int32), axis=0)
    offset = tok_index - seg_start + jnp.where(seg_row == 0, first_offset, 0).astype(jnp.int32)
    half_side = side_row // 2
    window = offset // 4
    corner = offset % 4
    return (2 * (window // half_side) + corner // 2, 2 * (window % half_side) + corner % 2)

def key_labels(seg_row, plan_row):
    row_len = seg_row.shape[0]
    tok_index = jnp.arange(row_len, dtype=jnp.int32)
    before = jnp.where(tok_index >= row_len - plan_row[0], 0, -1).astype(jnp.int32)
    after_keys = jnp.where(tok_index < plan_row[1], seg_row[row_len - 1], -1).astype(jnp.int32)
    return jnp.concatenate([before, seg_row.astype(jnp.int32), after_keys])

def rotate_pairs(channels, angles, axis_pos):
    quarter = channels.shape[axis_pos] // 2
    first_half = lax.slice_in_dim(channels, 0, quarter, axis=axis_pos)
    second_half = lax.slice_in_dim(channels, quarter, 2 * quarter, axis=axis_pos)
    cosine = jnp.cos(angles)
    sine_tab = jnp.sin(angles)
    return jnp.concatenate([first_half * cosine - second_half * sine_tab, second_half * cosine + first_half * sine_tab], axis=axis_pos)

def apply_rope(channels, row_angles, col_angles, axis_pos):
    half_width = channels.shape[axis_pos] // 2
    row_part = rotate_pairs(lax.slice_in_dim(channels, 0, half_width, axis=axis_pos), row_angles, axis_pos)
    col_part = rotate_pairs(lax.slice_in_dim(channels, half_width, 2 * half_width, axis=axis_pos), col_angles, axis_pos)
    return jnp.concatenate([row_part, col_part], axis=axis_pos)

def reference(patches, segment_ids, grid_sides, split_plan, owner_dev, dest_row, ln_gain, ln_bias, w_qkv, w_out, w_proj):
    row_patches = patches.reshape(N_REQ, TOK_DEV, D)
    row_segments = segment_ids.reshape(N_REQ, TOK_DEV)
    row_sides = grid_sides.reshape(N_REQ, TOK_DEV)
    quarter = HD // 4
    frequency = 10000.0 ** (-jnp.arange(quarter, dtype=jnp.float32) / quarter)
    w_flat = w_qkv.reshape(3 * D, D)

    def project_row(packed):
        patch_row, seg_row, side_row, plan_row = packed
        normed = layer_norm(patch_row, ln_gain, ln_bias)
        mixed_qkv = jnp.dot(normed, w_flat.T, preferred_element_type=jnp.float32).reshape(TOK_DEV, 3, HEADS, HD)
        grid_row, grid_col = grid_positions(seg_row, side_row, plan_row[0])
        row_angles = grid_row.astype(jnp.float32)[:, None, None] * frequency
        col_angles = grid_col.astype(jnp.float32)[:, None, None] * frequency
        queries = apply_rope(mixed_qkv[:, 0], row_angles, col_angles, 2).astype(jnp.bfloat16)
        key_rot = apply_rope(mixed_qkv[:, 1], row_angles, col_angles, 2).astype(jnp.bfloat16)
        return (queries, key_rot, mixed_qkv[:, 2].astype(jnp.bfloat16))
    queries, all_keys, all_values = lax.map(project_row, (row_patches, row_segments, row_sides, split_plan))
    pad_width = ((1, 1), (0, 0), (0, 0), (0, 0))
    keys_pad = jnp.pad(all_keys, pad_width)
    values_pad = jnp.pad(all_values, pad_width)
    group_width = D // HEAD_GROUPS
    w_groups = w_out.reshape(HEAD_GROUPS, group_width, D).astype(jnp.float32)

    def attend_row(packed):
        row_index, patch_row, query_row, seg_row, plan_row = packed
        near_keys = lax.dynamic_slice_in_dim(keys_pad, row_index, 3, 0).reshape(3 * TOK_DEV, HEADS, HD)
        near_values = lax.dynamic_slice_in_dim(values_pad, row_index, 3, 0).reshape(3 * TOK_DEV, HEADS, HD)
        labels = key_labels(seg_row, plan_row)
        allowed = seg_row[:, None] == labels[None, :]
        scores = jnp.einsum('qhc,khc->hqk', query_row.astype(jnp.float32), near_keys.astype(jnp.float32)) * HD ** (-0.5)
        scores = jnp.where(allowed[None], scores, -1e+30)
        largest = lax.optimization_barrier(jnp.max(scores, axis=-1, keepdims=True))
        weights = jnp.exp(scores - largest)
        attn_probs = (weights / lax.optimization_barrier(jnp.sum(weights, axis=-1, keepdims=True))).astype(jnp.bfloat16)
        heads_out = jnp.einsum('hqk,khc->qhc', attn_probs.astype(jnp.float32), near_values.astype(jnp.float32)).astype(jnp.bfloat16)
        grouped = heads_out.reshape(TOK_DEV, HEAD_GROUPS, group_width).astype(jnp.float32)
        partial_value = jnp.einsum('qgc,gcd->gqd', grouped, w_groups).astype(jnp.bfloat16)
        attn_sum = lax.optimization_barrier(jnp.sum(partial_value.astype(jnp.float32), axis=0))
        return (patch_row.astype(jnp.float32) + attn_sum).astype(jnp.bfloat16)
    mixed_rows = lax.map(attend_row, (jnp.arange(N_REQ, dtype=jnp.int32), row_patches, queries, row_segments, split_plan))
    merged = mixed_rows.reshape(MERGED, 4 * D)
    projected = jnp.dot(merged, w_proj, preferred_element_type=jnp.float32).astype(jnp.bfloat16)
    target = owner_dev * (TOK_DEV // 4) + dest_row
    return jnp.zeros((MERGED, PROJ), jnp.bfloat16).at[target].set(projected)
```

```python
import functools

import jax
import jax.numpy as jnp
import numpy as np
from jax import lax
from jax.experimental import pallas as pl
from jax.experimental.pallas import tpu as pltpu
from jax.sharding import PartitionSpec as P

HD = 88
QUARTER = HD // 4
SIDE_MAX = 32
AUG = 128
VAUG = 96
BIG = 1e30
TILE = 256
BLK = 256
F32 = jnp.float32
BF16 = jnp.bfloat16
NT = (((1,), (1,)), ((), ()))
NN = (((1,), (0,)), ((), ()))
TN = (((0,), (0,)), ((), ()))
LOG2E = 1.4426950408889634


def rope_table():
    freq = 10000.0 ** (-np.arange(QUARTER, dtype=np.float64) / QUARTER)
    chan = np.arange(HD)
    pos = np.arange(SIDE_MAX, dtype=np.float64)
    angle = freq[chan % QUARTER][:, None] * pos[None, :]
    sign = np.where(chan % (2 * QUARTER) < QUARTER, -1.0, 1.0)[:, None]
    in_row = (chan < 2 * QUARTER)[:, None]
    halves = []
    for part in (np.cos(angle), sign * np.sin(angle)):
        halves.append(np.concatenate([np.where(in_row, part, 0.0), np.where(in_row, 0.0, part)], axis=1))
    table = np.concatenate(halves, axis=0).astype(np.float32)
    terms = []
    for _ in range(3):
        term = table.astype(jnp.bfloat16)
        terms.append(term)
        table = table - term.astype(np.float32)
    return np.concatenate(terms, axis=1)


def seg_counts(seg):
    ids = lax.broadcasted_iota(jnp.int32, (16, seg.shape[1]), 0)
    below = jnp.sum((seg < ids).astype(F32), axis=1, keepdims=True)
    return below


def label_rows(label):
    ids = lax.broadcasted_iota(jnp.int32, (AUG - HD, label.shape[1]), 0)
    return (ids == jnp.where(label < 0, 16, label)).astype(F32)


def qkv_kernel(plan_ref, table_ref, seg_ref, segt_ref, side_ref, x_ref, gain_ref, bias_ref, w_ref, q_ref, kv_ref):
    heads = q_ref.shape[0]
    step = pl.program_id(0)
    x = x_ref[...].astype(F32)
    centred = x - jnp.mean(x, axis=1, keepdims=True)
    variance = jnp.mean(centred * centred, axis=1, keepdims=True)
    normed = (centred * lax.rsqrt(variance + 1e-6) * gain_ref[...] + bias_ref[...]).astype(BF16)

    below = seg_counts(seg_ref[...])
    seg = segt_ref[...]
    ids = lax.broadcasted_iota(jnp.int32, (16, TILE), 0)
    start = jnp.sum(jnp.where(ids == seg, below, 0.0), axis=0, keepdims=True).astype(jnp.int32)
    token = lax.broadcasted_iota(jnp.int32, (1, TILE), 1) + step * TILE
    offset = token - start + jnp.where(seg == 0, plan_ref[0, 0], 0)
    window = lax.shift_right_logical(offset, 2)
    corner = offset & 3
    half = lax.shift_right_logical(side_ref[...], 1)
    down = jnp.floor((window.astype(F32) + 0.5) / half.astype(F32)).astype(jnp.int32)
    grid_row = 2 * down + lax.shift_right_logical(corner, 1)
    grid_col = 2 * (window - down * half) + (corner & 1)
    pos = lax.broadcasted_iota(jnp.int32, (2 * SIDE_MAX, TILE), 0)
    hot = ((pos == grid_row) | (pos == grid_col + SIDE_MAX)).astype(F32).astype(BF16)
    hot = jnp.concatenate([hot, hot, hot], axis=0)
    angles = lax.dot_general(table_ref[...], hot, NN, preferred_element_type=F32)
    cosine, sine = angles[:HD], angles[HD:]
    first = lax.broadcasted_iota(jnp.int32, (HD, TILE), 0) % (2 * QUARTER) < QUARTER

    def rotated(value):
        partner = jnp.where(first, pltpu.roll(value, HD - QUARTER, 0), pltpu.roll(value, QUARTER, 0))
        return value * cosine + partner * sine

    aug = lax.broadcasted_iota(jnp.int32, (AUG - HD, TILE), 0)
    barred = jnp.where(aug == jnp.broadcast_to(seg, aug.shape), 0.0, jnp.where(aug <= 16, -BIG, 0.0))
    queries = lax.dot_general(w_ref[0], normed, NT, preferred_element_type=F32)
    keys = lax.dot_general(w_ref[1], normed, NT, preferred_element_type=F32)
    values = lax.dot_general(w_ref[2], normed, NT, preferred_element_type=F32)
    for h in range(heads):
        span = slice(h * HD, (h + 1) * HD)
        query = rotated(queries[span]) * (HD**-0.5 * LOG2E)
        q_ref[h] = jnp.concatenate([query, barred], axis=0).astype(BF16)
        kv_ref[0, h] = rotated(keys[span]).astype(BF16)
        kv_ref[1, h] = values[span].astype(BF16)


def qkv_call(patches, seg, sides, plan, gain, bias, w_qkv, table):
    count, width = patches.shape
    local = w_qkv.shape[1]
    heads = local // HD
    whole = lambda *shape: pl.BlockSpec(shape, lambda i: (0,) * len(shape))
    return pl.pallas_call(
        qkv_kernel,
        grid=(count // TILE,),
        in_specs=[
            pl.BlockSpec(memory_space=pltpu.SMEM),
            whole(*table.shape),
            whole(1, count),
            pl.BlockSpec((1, TILE), lambda i: (0, i)),
            pl.BlockSpec((1, TILE), lambda i: (0, i)),
            pl.BlockSpec((TILE, width), lambda i: (i, 0)),
            whole(1, width),
            whole(1, width),
            whole(3, local, width),
        ],
        out_specs=[
            pl.BlockSpec((heads, AUG, TILE), lambda i: (0, 0, i)),
            pl.BlockSpec((2, heads, HD, TILE), lambda i: (0, 0, 0, i)),
        ],
        out_shape=[
            jax.ShapeDtypeStruct((heads, AUG, count), BF16),
            jax.ShapeDtypeStruct((2, heads, HD, count), BF16),
        ],
        compiler_params=pltpu.CompilerParams(vmem_limit_bytes=48 << 20),
        cost_estimate=pl.CostEstimate(flops=6 * count * width * local, bytes_accessed=10 << 20, transcendentals=0),
        name="qkv",
    )(plan, table, seg, seg, sides, patches, gain, bias, w_qkv)


def prepare_block(kv_ref, label, keys, values, base):
    heads = keys.shape[0]
    rows = label_rows(label)
    extra = VAUG - HD
    ones = (lax.broadcasted_iota(jnp.int32, (extra, BLK), 0) == 0).astype(F32)
    for h in range(heads):
        block = jnp.concatenate([kv_ref[0, h, :, pl.ds(base, BLK)].astype(F32), rows], axis=0)
        keys[h, pl.ds(base, BLK), :] = block.T.astype(BF16)
        block = jnp.concatenate([kv_ref[1, h, :, pl.ds(base, BLK)].astype(F32), ones], axis=0)
        values[h, :, pl.ds(base, BLK)] = block.astype(BF16)


def attend(q_ref, keys, values, acc, top, q_base, k_base):
    heads = keys.shape[0]
    for h in range(heads):
        query = q_ref[h, :, pl.ds(q_base, BLK)]
        scores = lax.dot_general(keys[h, pl.ds(k_base, BLK), :], query, NN, preferred_element_type=F32)
        old = top[h : h + 1, pl.ds(q_base, BLK)]
        new = jnp.maximum(old, jnp.max(scores, axis=0, keepdims=True))
        weights = jnp.exp2(scores - new).astype(BF16)
        part = lax.dot_general(values[h, :, pl.ds(k_base, BLK)], weights, NN, preferred_element_type=F32)
        acc[h, :, pl.ds(q_base, BLK)] = acc[h, :, pl.ds(q_base, BLK)] * jnp.exp2(old - new) + part
        top[h : h + 1, pl.ds(q_base, BLK)] = new


def own_kernel(sseg_ref, seg_ref, q_ref, kv_ref, acc_ref, top_ref, keys, values):
    count = seg_ref.shape[1]
    seg = seg_ref[...]
    for b in range(count // BLK):
        prepare_block(kv_ref, seg[:, b * BLK : (b + 1) * BLK], keys, values, b * BLK)
    acc_ref[...] = jnp.zeros_like(acc_ref)
    top_ref[...] = jnp.full_like(top_ref, -BIG)

    def block(b, carry):
        q_base = pl.multiple_of(b * BLK, BLK)
        low = jnp.sum((seg < sseg_ref[0, q_base]).astype(jnp.int32))
        high = jnp.sum((seg <= sseg_ref[0, q_base + BLK - 1]).astype(jnp.int32))

        def inner(k, c):
            attend(q_ref, keys, values, acc_ref, top_ref, q_base, pl.multiple_of(k * BLK, BLK))
            return c

        return lax.fori_loop(low // BLK, (high + BLK - 1) // BLK, inner, carry)

    lax.fori_loop(0, count // BLK, block, 0)


def own_call(seg, q, kv):
    heads, _, count = q.shape
    vmem = pl.BlockSpec(memory_space=pltpu.VMEM)
    return pl.pallas_call(
        own_kernel,
        in_specs=[pl.BlockSpec(memory_space=pltpu.SMEM), vmem, vmem, vmem],
        out_specs=[vmem, vmem],
        out_shape=[
            jax.ShapeDtypeStruct((heads, VAUG, count), F32),
            jax.ShapeDtypeStruct((8, count), F32),
        ],
        scratch_shapes=[pltpu.VMEM((heads, count, AUG), BF16), pltpu.VMEM((heads, VAUG, count), BF16)],
        compiler_params=pltpu.CompilerParams(vmem_limit_bytes=48 << 20),
        cost_estimate=pl.CostEstimate(flops=8 << 30, bytes_accessed=8 << 20, transcendentals=4 << 20),
        name="own_keys",
    )(seg, seg, q, kv)


def halo_kernel(plan_ref, sseg_ref, q_ref, acc_in, top_in, before_ref, after_ref, out_ref, acc, top, keys, values):
    heads, _, count = q_ref.shape
    acc[...] = acc_in[...]
    top[...] = top_in[...]
    lead, trail = plan_ref[0, 0], plan_ref[0, 1]
    last = sseg_ref[0, count - 1]
    token = lax.broadcasted_iota(jnp.int32, (1, BLK), 1)

    def before_block(k, carry):
        base = pl.multiple_of(k * BLK, BLK)
        label = jnp.where(token + base >= count - lead, 0, -1)
        prepare_block(before_ref, label, keys, values, base)

        def inner(b, c):
            q_base = pl.multiple_of(b * BLK, BLK)

            @pl.when(sseg_ref[0, q_base] == 0)
            def _():
                attend(q_ref, keys, values, acc, top, q_base, base)

            return c

        return lax.fori_loop(0, count // BLK, inner, carry)

    lax.fori_loop((count - lead) // BLK, count // BLK, before_block, 0)

    def after_block(k, carry):
        base = pl.multiple_of(k * BLK, BLK)
        label = jnp.where(token + base < trail, last, -1)
        prepare_block(after_ref, label, keys, values, base)

        def inner(b, c):
            q_base = pl.multiple_of(b * BLK, BLK)

            @pl.when(sseg_ref[0, q_base + BLK - 1] == last)
            def _():
                attend(q_ref, keys, values, acc, top, q_base, base)

            return c

        return lax.fori_loop(0, count // BLK, inner, carry)

    lax.fori_loop(0, (trail + BLK - 1) // BLK, after_block, 0)
    for h in range(heads):
        out_ref[pl.ds(h * HD, HD), :] = (acc[h, :HD, :] / acc[h, HD : HD + 1, :]).astype(BF16)


def halo_call(plan, seg, q, acc, top, before, after):
    heads, _, count = q.shape
    vmem = pl.BlockSpec(memory_space=pltpu.VMEM)
    smem = pl.BlockSpec(memory_space=pltpu.SMEM)
    return pl.pallas_call(
        halo_kernel,
        in_specs=[smem, smem, vmem, vmem, vmem, vmem, vmem],
        out_specs=vmem,
        out_shape=jax.ShapeDtypeStruct((heads * HD, count), BF16),
        scratch_shapes=[
            pltpu.VMEM(acc.shape, F32),
            pltpu.VMEM(top.shape, F32),
            pltpu.VMEM((heads, count, AUG), BF16),
            pltpu.VMEM((heads, VAUG, count), BF16),
        ],
        compiler_params=pltpu.CompilerParams(vmem_limit_bytes=48 << 20),
        cost_estimate=pl.CostEstimate(flops=8 << 30, bytes_accessed=8 << 20, transcendentals=4 << 20),
        name="halo_keys",
    )(plan, seg, q, acc, top, before, after)


def out_kernel(slot_ref, dest_ref, x_ref, own_ref, left_ref, right_ref, far_ref, w_own, w_left, w_right, w_far, proj_hbm, send_ref, mixed, proj, sem):
    step = pl.program_id(0)
    width = x_ref.shape[1]
    copy = pltpu.make_async_copy(proj_hbm, proj, sem)

    @pl.when(step == 0)
    def _():
        copy.start()

    total = x_ref[...].astype(F32)
    for h_ref, w_ref in ((own_ref, w_own), (left_ref, w_left), (right_ref, w_right), (far_ref, w_far)):
        total += lax.dot_general(h_ref[...], w_ref[...], TN, preferred_element_type=F32)
    chunks = width // 128
    base = pl.multiple_of(step * TILE, TILE)
    for c in range(chunks):
        mixed[c, pl.ds(base, TILE), :] = total[:, c * 128 : (c + 1) * 128]

    @pl.when(step == pl.num_programs(0) - 1)
    def _():
        copy.wait()
        rows = mixed.shape[1] // 4
        result = jnp.zeros((rows, proj.shape[1]), F32)
        for j in range(4):
            part = jnp.concatenate([mixed[c, pl.ds(j, rows, stride=4), :] for c in range(chunks)], axis=1).astype(BF16)
            result += lax.dot_general(part, proj[j * width : (j + 1) * width, :], NN, preferred_element_type=F32)
        slots = lax.broadcasted_iota(jnp.int32, (send_ref.shape[0], rows), 0)
        pick = (slots == slot_ref[...]).astype(F32)
        cols = proj.shape[1]
        send_ref[:, :cols] = lax.dot_general(
            pick.astype(BF16), result.astype(BF16), NN, preferred_element_type=F32
        ).astype(BF16)
        dest = jnp.sum(pick * dest_ref[...].astype(F32), axis=1, keepdims=True)
        send_ref[:, cols:] = jnp.broadcast_to(dest, (send_ref.shape[0], 128)).astype(BF16)


def out_call(slot, dest, patches, heads_parts, w_parts, w_proj, slots):
    count, width = patches.shape
    local = heads_parts[0].shape[0]
    cols = w_proj.shape[1]
    whole = lambda *shape: pl.BlockSpec(shape, lambda i: (0,) * len(shape))
    return pl.pallas_call(
        out_kernel,
        grid=(count // TILE,),
        in_specs=[whole(*slot.shape), whole(*dest.shape), pl.BlockSpec((TILE, width), lambda i: (i, 0))]
        + [pl.BlockSpec((local, TILE), lambda i: (0, i))] * 4
        + [whole(local, width)] * 4
        + [pl.BlockSpec(memory_space=pl.ANY)],
        out_specs=whole(slots, cols + 128),
        out_shape=jax.ShapeDtypeStruct((slots, cols + 128), BF16),
        scratch_shapes=[
            pltpu.VMEM((width // 128, count, 128), F32),
            pltpu.VMEM(w_proj.shape, BF16),
            pltpu.SemaphoreType.DMA,
        ],
        compiler_params=pltpu.CompilerParams(vmem_limit_bytes=56 << 20),
        cost_estimate=pl.CostEstimate(flops=6 << 30, bytes_accessed=18 << 20, transcendentals=0),
        name="project",
    )(slot, dest, patches, *heads_parts, *w_parts, w_proj)


def place_kernel(got_ref, out_ref):
    cols = out_ref.shape[1]
    dest = got_ref[:, cols:].astype(F32).astype(jnp.int32)
    dest = jnp.concatenate([dest] * (out_ref.shape[0] // 128), axis=1)
    rows = lax.broadcasted_iota(jnp.int32, dest.shape, 1)
    pick = (rows == dest).astype(F32).astype(BF16)
    out_ref[...] = lax.dot_general(pick, got_ref[:, :cols], TN, preferred_element_type=F32).astype(BF16)


def place_call(got, rows, cols):
    vmem = pl.BlockSpec(memory_space=pltpu.VMEM)
    return pl.pallas_call(
        place_kernel,
        in_specs=[vmem],
        out_specs=vmem,
        out_shape=jax.ShapeDtypeStruct((rows, cols), BF16),
        name="place",
    )(got)


def ring(axis, shift):
    size = lax.axis_size(axis)
    return [(i, (i + shift) % size) for i in range(size)]


def around(block, axis):
    half = block.shape[0] // 2
    left = lax.ppermute(block, axis, ring(axis, 1))
    right = lax.ppermute(block, axis, ring(axis, -1))
    far = jnp.concatenate(
        [
            lax.ppermute(left[:half], axis, ring(axis, 1)),
            lax.ppermute(right[half:], axis, ring(axis, -1)),
        ],
        axis=0,
    )
    return [block, left, right, far]


def on_device(patches, segment_ids, grid_sides, split_plan, owner_dev, dest_row, ln_gain, ln_bias, w_qkv, w_out, w_proj):
    count, width = patches.shape
    rows_out = owner_dev.shape[0]
    peers = lax.axis_size("req")
    lanes = 2 * rows_out // peers
    seg = segment_ids.reshape(1, count)
    table = jnp.asarray(rope_table())
    w_parts = around(w_out, "tp")
    q, kv = qkv_call(
        patches, seg, grid_sides.reshape(1, count), split_plan, ln_gain.reshape(1, width), ln_bias.reshape(1, width), w_qkv, table
    )
    up = [(i, i + 1) for i in range(peers - 1)]
    down = [(j, i) for i, j in up]
    before = lax.ppermute(kv, "req", up)
    after = lax.ppermute(kv, "req", down)
    acc, top = own_call(seg, q, kv)
    heads_out = halo_call(split_plan, seg, q, acc, top, before, after)
    heads_parts = around(heads_out, "tp")
    within = jnp.arange(rows_out, dtype=jnp.int32) % lanes
    slot = (owner_dev * lanes + within).reshape(1, rows_out)
    send = out_call(slot, dest_row.reshape(1, rows_out), patches, heads_parts, w_parts, w_proj, peers * lanes)
    cols = send.shape[1]
    got = lax.all_to_all(send.reshape(peers, lanes, cols), "req", split_axis=0, concat_axis=0, tiled=True)
    return place_call(got.reshape(peers * lanes, cols), rows_out, w_proj.shape[1])


def solution(mesh):
    placed = (
        P("req", None),
        P("req"),
        P("req"),
        P("req", None),
        P("req"),
        P("req"),
        P(),
        P(),
        P(None, "tp", None),
        P("tp", None),
        P(None, "tp"),
    )
    return jax.shard_map(on_device, mesh=mesh, in_specs=placed, out_specs=P("req", "tp"), check_vma=False)
```

```python
import functools

import jax
import jax.numpy as jnp
import numpy as np
from jax import lax
from jax.experimental import pallas as pl
from jax.experimental.pallas import tpu as pltpu
from jax.sharding import PartitionSpec as P

HD = 88
QUARTER = HD // 4
SIDE_MAX = 32
AUG = 128
VAUG = 96
BIG = 1e30
TILE = 256
QB = 512
KB = 256
F32 = jnp.float32
BF16 = jnp.bfloat16
NT = (((1,), (1,)), ((), ()))
NN = (((1,), (0,)), ((), ()))
TN = (((0,), (0,)), ((), ()))
LOG2E = 1.4426950408889634


def rope_table():
    freq = 10000.0 ** (-np.arange(QUARTER, dtype=np.float64) / QUARTER)
    chan = np.arange(HD)
    pos = np.arange(SIDE_MAX, dtype=np.float64)
    angle = freq[chan % QUARTER][:, None] * pos[None, :]
    sign = np.where(chan % (2 * QUARTER) < QUARTER, -1.0, 1.0)[:, None]
    in_row = (chan < 2 * QUARTER)[:, None]
    halves = []
    for part in (np.cos(angle), sign * np.sin(angle)):
        halves.append(np.concatenate([np.where(in_row, part, 0.0), np.where(in_row, 0.0, part)], axis=1))
    table = np.concatenate(halves, axis=0).astype(np.float32)
    terms = []
    for _ in range(3):
        term = table.astype(jnp.bfloat16)
        terms.append(term)
        table = table - term.astype(np.float32)
    return np.concatenate(terms, axis=1)


def seg_counts(seg):
    ids = lax.broadcasted_iota(jnp.int32, (16, seg.shape[1]), 0)
    below = jnp.sum((seg < ids).astype(F32), axis=1, keepdims=True)
    return below


def label_rows(label):
    ids = lax.broadcasted_iota(jnp.int32, (AUG - HD, label.shape[1]), 0)
    return (ids == jnp.where(label < 0, 16, label)).astype(F32)


def qkv_kernel(plan_ref, table_ref, seg_ref, segt_ref, side_ref, x_ref, gain_ref, bias_ref, w_ref, q_ref, kv_ref):
    heads = q_ref.shape[0]
    step = pl.program_id(0)
    x = x_ref[...].astype(F32)
    centred = x - jnp.mean(x, axis=1, keepdims=True)
    variance = jnp.mean(centred * centred, axis=1, keepdims=True)
    normed = (centred * lax.rsqrt(variance + 1e-6) * gain_ref[...].reshape(1, -1) + bias_ref[...].reshape(1, -1)).astype(BF16)

    below = seg_counts(seg_ref[...])
    seg = segt_ref[...]
    ids = lax.broadcasted_iota(jnp.int32, (16, TILE), 0)
    start = jnp.sum(jnp.where(ids == seg, below, 0.0), axis=0, keepdims=True).astype(jnp.int32)
    token = lax.broadcasted_iota(jnp.int32, (1, TILE), 1) + step * TILE
    offset = token - start + jnp.where(seg == 0, plan_ref[0, 0], 0)
    window = lax.shift_right_logical(offset, 2)
    corner = offset & 3
    half = lax.shift_right_logical(side_ref[...], 1)
    down = jnp.floor((window.astype(F32) + 0.5) / half.astype(F32)).astype(jnp.int32)
    grid_row = 2 * down + lax.shift_right_logical(corner, 1)
    grid_col = 2 * (window - down * half) + (corner & 1)
    pos = lax.broadcasted_iota(jnp.int32, (2 * SIDE_MAX, TILE), 0)
    hot = ((pos == grid_row) | (pos == grid_col + SIDE_MAX)).astype(F32).astype(BF16)
    hot = jnp.concatenate([hot, hot, hot], axis=0)
    angles = lax.dot_general(table_ref[...], hot, NN, preferred_element_type=F32)
    cosine, sine = angles[:HD], angles[HD:]
    first = lax.broadcasted_iota(jnp.int32, (HD, TILE), 0) % (2 * QUARTER) < QUARTER

    def rotated(value):
        partner = jnp.where(first, pltpu.roll(value, HD - QUARTER, 0), pltpu.roll(value, QUARTER, 0))
        return value * cosine + partner * sine

    aug = lax.broadcasted_iota(jnp.int32, (AUG - HD, TILE), 0)
    barred = jnp.where(aug == jnp.broadcast_to(seg, aug.shape), 0.0, jnp.where(aug <= 16, -BIG, 0.0))
    queries = lax.dot_general(w_ref[0], normed, NT, preferred_element_type=F32)
    keys = lax.dot_general(w_ref[1], normed, NT, preferred_element_type=F32)
    values = lax.dot_general(w_ref[2], normed, NT, preferred_element_type=F32)
    for h in range(heads):
        span = slice(h * HD, (h + 1) * HD)
        query = rotated(queries[span]) * (HD**-0.5 * LOG2E)
        q_ref[h] = jnp.concatenate([query, barred], axis=0).astype(BF16)
        kv_ref[0, h] = rotated(keys[span]).astype(BF16)
        kv_ref[1, h] = values[span].astype(BF16)


def qkv_call(patches, seg, sides, plan, gain, bias, w_qkv, table):
    count, width = patches.shape
    local = w_qkv.shape[1]
    heads = local // HD
    whole = lambda *shape: pl.BlockSpec(shape, lambda i: (0,) * len(shape))
    return pl.pallas_call(
        qkv_kernel,
        grid=(count // TILE,),
        in_specs=[
            pl.BlockSpec(memory_space=pltpu.SMEM),
            whole(*table.shape),
            whole(1, count),
            pl.BlockSpec((1, TILE), lambda i: (0, i)),
            pl.BlockSpec((1, TILE), lambda i: (0, i)),
            pl.BlockSpec((TILE, width), lambda i: (i, 0)),
            whole(width),
            whole(width),
            whole(3, local, width),
        ],
        out_specs=[
            pl.BlockSpec((heads, AUG, TILE), lambda i: (0, 0, i)),
            pl.BlockSpec((2, heads, HD, TILE), lambda i: (0, 0, 0, i)),
        ],
        out_shape=[
            jax.ShapeDtypeStruct((heads, AUG, count), BF16),
            jax.ShapeDtypeStruct((2, heads, HD, count), BF16),
        ],
        compiler_params=pltpu.CompilerParams(vmem_limit_bytes=30 << 20),
        cost_estimate=pl.CostEstimate(flops=6 * count * width * local, bytes_accessed=10 << 20, transcendentals=0),
        name="qkv",
    )(*[pltpu.with_memory_space_constraint(v, pltpu.HBM) for v in (plan, table, seg, seg, sides, patches, gain, bias, w_qkv)])


def prepare_block(kv_ref, label, keys, values, base):
    heads = keys.shape[0]
    rows = label_rows(label)
    extra = VAUG - HD
    ones = (lax.broadcasted_iota(jnp.int32, (extra, KB), 0) == 0).astype(F32)
    for h in range(heads):
        block = jnp.concatenate([kv_ref[0, h, :, pl.ds(base, KB)].astype(F32), rows], axis=0)
        keys[h, pl.ds(base, KB), :] = block.astype(BF16).T
        block = jnp.concatenate([kv_ref[1, h, :, pl.ds(base, KB)].astype(F32), ones], axis=0)
        values[h, :, pl.ds(base, KB)] = block.astype(BF16)


def attend(q_ref, keys, values, acc, top, q_base, k_base):
    heads = keys.shape[0]
    span = pl.ds(q_base, QB)
    old = [top[h : h + 1, span] for h in range(heads)]
    scores = [
        lax.dot_general(keys[h, pl.ds(k_base, KB), :], q_ref[h, :, span], NN, preferred_element_type=F32)
        for h in range(heads)
    ]
    new = [jnp.maximum(old[h], jnp.max(scores[h], axis=0, keepdims=True)) for h in range(heads)]
    weights = [jnp.exp2(scores[h] - new[h]).astype(BF16) for h in range(heads)]
    parts = [
        lax.dot_general(values[h, :, pl.ds(k_base, KB)], weights[h], NN, preferred_element_type=F32)
        for h in range(heads)
    ]
    sums = [acc[h, :, span] * jnp.exp2(old[h] - new[h]) + parts[h] for h in range(heads)]
    for h in range(heads):
        acc[h, :, span] = sums[h]
        top[h : h + 1, span] = new[h]


def own_kernel(sseg_ref, seg_ref, q_ref, kv_ref, acc_ref, top_ref, keys, values):
    count = seg_ref.shape[1]
    seg = seg_ref[...]
    for b in range(count // KB):
        prepare_block(kv_ref, seg[:, b * KB : (b + 1) * KB], keys, values, b * KB)
    acc_ref[...] = jnp.zeros_like(acc_ref)
    top_ref[...] = jnp.full_like(top_ref, -BIG)

    def block(b, carry):
        q_base = pl.multiple_of(b * QB, QB)
        low = jnp.sum((seg < sseg_ref[0, q_base]).astype(jnp.int32))
        high = jnp.sum((seg <= sseg_ref[0, q_base + QB - 1]).astype(jnp.int32))

        def inner(k, c):
            attend(q_ref, keys, values, acc_ref, top_ref, q_base, pl.multiple_of(k * KB, KB))
            return c

        return lax.fori_loop(low // KB, (high + KB - 1) // KB, inner, carry)

    lax.fori_loop(0, count // QB, block, 0)


def own_call(seg, q, kv):
    heads, _, count = q.shape
    vmem = pl.BlockSpec(memory_space=pltpu.VMEM)
    return pl.pallas_call(
        own_kernel,
        in_specs=[pl.BlockSpec(memory_space=pltpu.SMEM), vmem, vmem, vmem],
        out_specs=[vmem, vmem],
        out_shape=[
            jax.ShapeDtypeStruct((heads, VAUG, count), F32),
            jax.ShapeDtypeStruct((8, count), F32),
        ],
        scratch_shapes=[pltpu.VMEM((heads, count, AUG), BF16), pltpu.VMEM((heads, VAUG, count), BF16)],
        compiler_params=pltpu.CompilerParams(vmem_limit_bytes=20 << 20),
        cost_estimate=pl.CostEstimate(flops=8 << 30, bytes_accessed=8 << 20, transcendentals=4 << 20),
        name="own_keys",
    )(seg, seg, q, kv)


def halo_kernel(plan_ref, sseg_ref, q_ref, acc_in, top_in, before_ref, after_ref, out_ref, acc, top, keys, values):
    heads, _, count = q_ref.shape
    acc[...] = acc_in[...]
    top[...] = top_in[...]
    lead, trail = plan_ref[0, 0], plan_ref[0, 1]
    last = sseg_ref[0, count - 1]
    token = lax.broadcasted_iota(jnp.int32, (1, KB), 1)

    def before_block(k, carry):
        base = pl.multiple_of(k * KB, KB)
        label = jnp.where(token + base >= count - lead, 0, -1)
        prepare_block(before_ref, label, keys, values, base)

        def inner(b, c):
            q_base = pl.multiple_of(b * QB, QB)

            @pl.when(sseg_ref[0, q_base] == 0)
            def _():
                attend(q_ref, keys, values, acc, top, q_base, base)

            return c

        return lax.fori_loop(0, count // QB, inner, carry)

    lax.fori_loop((count - lead) // KB, count // KB, before_block, 0)

    def after_block(k, carry):
        base = pl.multiple_of(k * KB, KB)
        label = jnp.where(token + base < trail, last, -1)
        prepare_block(after_ref, label, keys, values, base)

        def inner(b, c):
            q_base = pl.multiple_of(b * QB, QB)

            @pl.when(sseg_ref[0, q_base + QB - 1] == last)
            def _():
                attend(q_ref, keys, values, acc, top, q_base, base)

            return c

        return lax.fori_loop(0, count // QB, inner, carry)

    lax.fori_loop(0, (trail + KB - 1) // KB, after_block, 0)
    for h in range(heads):
        out_ref[pl.ds(h * HD, HD), :] = (acc[h, :HD, :] / acc[h, HD : HD + 1, :]).astype(BF16)


def halo_call(plan, seg, q, acc, top, before, after):
    heads, _, count = q.shape
    vmem = pl.BlockSpec(memory_space=pltpu.VMEM)
    smem = pl.BlockSpec(memory_space=pltpu.SMEM)
    return pl.pallas_call(
        halo_kernel,
        in_specs=[smem, smem, vmem, vmem, vmem, vmem, vmem],
        out_specs=vmem,
        out_shape=jax.ShapeDtypeStruct((heads * HD, count), BF16),
        scratch_shapes=[
            pltpu.VMEM(acc.shape, F32),
            pltpu.VMEM(top.shape, F32),
            pltpu.VMEM((heads, count, AUG), BF16),
            pltpu.VMEM((heads, VAUG, count), BF16),
        ],
        compiler_params=pltpu.CompilerParams(vmem_limit_bytes=20 << 20),
        cost_estimate=pl.CostEstimate(flops=8 << 30, bytes_accessed=8 << 20, transcendentals=4 << 20),
        name="halo_keys",
    )(plan, seg, q, acc, top, before, after)


def gather_kernel(parts, base_ref, *refs):
    out_ref = refs[-1]
    for start in range(0, out_ref.shape[0], TILE):
        span = slice(start, start + TILE)
        total = base_ref[span].astype(F32)
        for h_ref, w_ref in zip(refs[:parts], refs[parts : 2 * parts]):
            total += lax.dot_general(h_ref[:, span], w_ref[...], TN, preferred_element_type=F32)
        out_ref[span] = total


def gather_call(base, heads_parts, w_parts):
    vmem = pl.BlockSpec(memory_space=pltpu.VMEM)
    parts = len(heads_parts)
    flops = 2 * base.shape[0] * base.shape[1] * sum(h.shape[0] for h in heads_parts)
    return pl.pallas_call(
        functools.partial(gather_kernel, parts),
        in_specs=[vmem] * (1 + 2 * parts),
        out_specs=vmem,
        out_shape=jax.ShapeDtypeStruct(base.shape, F32),
        compiler_params=pltpu.CompilerParams(vmem_limit_bytes=16 << 20),
        cost_estimate=pl.CostEstimate(flops=flops, bytes_accessed=4 << 20, transcendentals=0),
        name="output",
    )(base, *heads_parts, *w_parts)


def project_kernel(parts, slot_ref, dest_ref, base_ref, *refs):
    proj, send_ref, mixed = refs[2 * parts :]
    count, width = base_ref.shape
    chunks = width // 128
    for start in range(0, count, TILE):
        span = slice(start, start + TILE)
        total = base_ref[span]
        for h_ref, w_ref in zip(refs[:parts], refs[parts : 2 * parts]):
            total += lax.dot_general(h_ref[:, span], w_ref[...], TN, preferred_element_type=F32)
        for c in range(chunks):
            mixed[c, span, :] = total[:, c * 128 : (c + 1) * 128]
    rows = count // 4
    result = jnp.zeros((rows, proj.shape[1]), F32)
    for j in range(4):
        part = jnp.concatenate([mixed[c, pl.ds(j, rows, stride=4), :] for c in range(chunks)], axis=1).astype(BF16)
        result += lax.dot_general(part, proj[j * width : (j + 1) * width, :], NN, preferred_element_type=F32)
    slots = lax.broadcasted_iota(jnp.int32, (send_ref.shape[0], rows), 0)
    pick = (slots == slot_ref[...]).astype(F32)
    cols = proj.shape[1]
    send_ref[:, :cols] = lax.dot_general(
        pick.astype(BF16), result.astype(BF16), NN, preferred_element_type=F32
    ).astype(BF16)
    dest = jnp.sum(pick * dest_ref[...].astype(F32), axis=1, keepdims=True)
    send_ref[:, cols:] = jnp.broadcast_to(dest, (send_ref.shape[0], 128)).astype(BF16)


def project_call(slot, dest, base, heads_parts, w_parts, w_proj, slots):
    vmem = pl.BlockSpec(memory_space=pltpu.VMEM)
    parts = len(heads_parts)
    count, width = base.shape
    cols = w_proj.shape[1]
    return pl.pallas_call(
        functools.partial(project_kernel, parts),
        in_specs=[vmem] * (4 + 2 * parts),
        out_specs=vmem,
        out_shape=jax.ShapeDtypeStruct((slots, cols + 128), BF16),
        scratch_shapes=[pltpu.VMEM((width // 128, count, 128), F32)],
        compiler_params=pltpu.CompilerParams(vmem_limit_bytes=24 << 20),
        cost_estimate=pl.CostEstimate(flops=3 << 30, bytes_accessed=8 << 20, transcendentals=0),
        name="project",
    )(slot, dest, base, *heads_parts, *w_parts, w_proj)


def place_kernel(got_ref, out_ref):
    cols = out_ref.shape[1]
    dest = got_ref[:, cols:].astype(F32).astype(jnp.int32)
    dest = jnp.concatenate([dest] * (out_ref.shape[0] // 128), axis=1)
    rows = lax.broadcasted_iota(jnp.int32, dest.shape, 1)
    pick = (rows == dest).astype(F32).astype(BF16)
    out_ref[...] = lax.dot_general(pick, got_ref[:, :cols], TN, preferred_element_type=F32).astype(BF16)


def place_call(got, rows, cols):
    vmem = pl.BlockSpec(memory_space=pltpu.VMEM)
    return pl.pallas_call(
        place_kernel,
        in_specs=[vmem],
        out_specs=vmem,
        out_shape=jax.ShapeDtypeStruct((rows, cols), BF16),
        name="place",
    )(got)


def ring(axis, shift):
    size = lax.axis_size(axis)
    return [(i, (i + shift) % size) for i in range(size)]


def around(block, axis):
    half = block.shape[0] // 2
    left = lax.ppermute(block, axis, ring(axis, 1))
    right = lax.ppermute(block, axis, ring(axis, -1))
    far_top = lax.ppermute(left[:half], axis, ring(axis, 1))
    far_end = lax.ppermute(right[half:], axis, ring(axis, -1))
    return left, right, far_top, far_end


def on_device(patches, segment_ids, grid_sides, split_plan, owner_dev, dest_row, ln_gain, ln_bias, w_qkv, w_out, w_proj):
    count, width = patches.shape
    rows_out = owner_dev.shape[0]
    peers = lax.axis_size("req")
    lanes = 2 * rows_out // peers
    seg = segment_ids.reshape(1, count)
    table = jnp.asarray(rope_table())
    w_left, w_right, w_top, w_end = around(w_out, "tp")
    q, kv = qkv_call(
        patches, seg, grid_sides.reshape(1, count), split_plan, ln_gain, ln_bias, w_qkv, table
    )
    up = [(i, i + 1) for i in range(peers - 1)]
    down = [(j, i) for i, j in up]
    before = lax.ppermute(kv, "req", up)
    after = lax.ppermute(kv, "req", down)
    acc, top = own_call(seg, q, kv)
    before, after, w_left, w_right, w_top, w_end = lax.optimization_barrier(
        (before, after, w_left, w_right, w_top, w_end)
    )
    heads_out = halo_call(split_plan, seg, q, acc, top, before, after)
    left, right, far_top, far_end = around(heads_out, "tp")
    within = jnp.arange(rows_out, dtype=jnp.int32) % lanes
    slot = (owner_dev * lanes + within).reshape(1, rows_out)
    base = gather_call(patches, [heads_out], [w_out])
    base = gather_call(base, [left, right], [w_left, w_right])
    send = project_call(
        slot, dest_row.reshape(1, rows_out), base, [far_top, far_end], [w_top, w_end], w_proj, peers * lanes
    )
    cols = send.shape[1]
    got = lax.all_to_all(send.reshape(peers, lanes, cols), "req", split_axis=0, concat_axis=0, tiled=True)
    return place_call(got.reshape(peers * lanes, cols), rows_out, w_proj.shape[1])


def solution(mesh):
    placed = (
        P("req", None),
        P("req"),
        P("req"),
        P("req", None),
        P("req"),
        P("req"),
        P(),
        P(),
        P(None, "tp", None),
        P("tp", None),
        P(None, "tp"),
    )
    return jax.shard_map(on_device, mesh=mesh, in_specs=placed, out_specs=P("req", "tp"), check_vma=False)
```

```python
import functools

import jax
import jax.numpy as jnp
import numpy as np
from jax import lax
from jax.experimental import pallas as pl
from jax.experimental.pallas import tpu as pltpu
from jax.sharding import PartitionSpec as P

HD = 88
QUARTER = HD // 4
SIDE_MAX = 32
AUG = 128
VAUG = 96
BIG = 1e30
TILE = 256
QB = 512
KB = 256
PACK = 2
F32 = jnp.float32
BF16 = jnp.bfloat16
NT = (((1,), (1,)), ((), ()))
NN = (((1,), (0,)), ((), ()))
TN = (((0,), (0,)), ((), ()))
LOG2E = 1.4426950408889634


def rope_table():
    freq = 10000.0 ** (-np.arange(QUARTER, dtype=np.float64) / QUARTER)
    chan = np.arange(HD)
    pos = np.arange(SIDE_MAX, dtype=np.float64)
    angle = freq[chan % QUARTER][:, None] * pos[None, :]
    sign = np.where(chan % (2 * QUARTER) < QUARTER, -1.0, 1.0)[:, None]
    in_row = (chan < 2 * QUARTER)[:, None]
    halves = []
    for part in (np.cos(angle), sign * np.sin(angle)):
        halves.append(np.concatenate([np.where(in_row, part, 0.0), np.where(in_row, 0.0, part)], axis=1))
    table = np.concatenate(halves, axis=0).astype(np.float32)
    terms = []
    for _ in range(3):
        term = table.astype(jnp.bfloat16)
        terms.append(term)
        table = table - term.astype(np.float32)
    return np.concatenate(terms, axis=1)


def seg_counts(seg):
    ids = lax.broadcasted_iota(jnp.int32, (16, seg.shape[1]), 0)
    below = jnp.sum((seg < ids).astype(F32), axis=1, keepdims=True)
    return below


def label_rows(label):
    ids = lax.broadcasted_iota(jnp.int32, (AUG - HD, label.shape[1]), 0)
    return (ids == jnp.where(label < 0, 16, label)).astype(F32)


def normalised(x_ref, gain_ref, bias_ref):
    x = x_ref[...].astype(F32)
    centred = x - jnp.mean(x, axis=1, keepdims=True)
    variance = jnp.mean(centred * centred, axis=1, keepdims=True)
    scaled = centred * lax.rsqrt(variance + 1e-6) * gain_ref[...].reshape(1, -1) + bias_ref[...].reshape(1, -1)
    return scaled.astype(BF16)


def rotations(plan_ref, table_ref, seg_ref, segt_ref, side_ref):
    below = seg_counts(seg_ref[...])
    seg = segt_ref[...]
    ids = lax.broadcasted_iota(jnp.int32, (16, TILE), 0)
    start = jnp.sum(jnp.where(ids == seg, below, 0.0), axis=0, keepdims=True).astype(jnp.int32)
    token = lax.broadcasted_iota(jnp.int32, (1, TILE), 1) + pl.program_id(0) * TILE
    offset = token - start + jnp.where(seg == 0, plan_ref[0, 0], 0)
    window = lax.shift_right_logical(offset, 2)
    corner = offset & 3
    half = lax.shift_right_logical(side_ref[...], 1)
    down = jnp.floor((window.astype(F32) + 0.5) / half.astype(F32)).astype(jnp.int32)
    grid_row = 2 * down + lax.shift_right_logical(corner, 1)
    grid_col = 2 * (window - down * half) + (corner & 1)
    pos = lax.broadcasted_iota(jnp.int32, (2 * SIDE_MAX, TILE), 0)
    hot = ((pos == grid_row) | (pos == grid_col + SIDE_MAX)).astype(F32).astype(BF16)
    hot = jnp.concatenate([hot, hot, hot], axis=0)
    angles = lax.dot_general(table_ref[...], hot, NN, preferred_element_type=F32)
    cosine, sine = angles[:HD], angles[HD:]
    first = lax.broadcasted_iota(jnp.int32, (HD, TILE), 0) % (2 * QUARTER) < QUARTER

    def rotated(value):
        partner = jnp.where(first, pltpu.roll(value, HD - QUARTER, 0), pltpu.roll(value, QUARTER, 0))
        return value * cosine + partner * sine

    return rotated


def kv_kernel(plan_ref, table_ref, seg_ref, segt_ref, side_ref, x_ref, gain_ref, bias_ref, wk_ref, wv_ref, *kv_refs):
    normed = normalised(x_ref, gain_ref, bias_ref)
    rotated = rotations(plan_ref, table_ref, seg_ref, segt_ref, side_ref)
    keys = lax.dot_general(wk_ref[0], normed, NT, preferred_element_type=F32)
    values = lax.dot_general(wv_ref[0], normed, NT, preferred_element_type=F32)
    pack = kv_refs[0].shape[1]
    for h in range(pack * len(kv_refs)):
        span = slice(h * HD, (h + 1) * HD)
        kv_refs[h // pack][0, h % pack] = rotated(keys[span]).astype(BF16)
        kv_refs[h // pack][1, h % pack] = values[span].astype(BF16)


def q_kernel(plan_ref, table_ref, seg_ref, segt_ref, side_ref, x_ref, gain_ref, bias_ref, w_ref, q_ref):
    normed = normalised(x_ref, gain_ref, bias_ref)
    rotated = rotations(plan_ref, table_ref, seg_ref, segt_ref, side_ref)
    queries = lax.dot_general(w_ref[0], normed, NT, preferred_element_type=F32)
    aug = lax.broadcasted_iota(jnp.int32, (AUG - HD, TILE), 0)
    barred = jnp.where(aug == jnp.broadcast_to(segt_ref[...], aug.shape), 0.0, jnp.where(aug <= 16, -BIG, 0.0))
    for h in range(q_ref.shape[0]):
        query = rotated(queries[h * HD : (h + 1) * HD]) * (HD**-0.5 * LOG2E)
        q_ref[h] = jnp.concatenate([query, barred], axis=0).astype(BF16)


def qkv_call(kernel, name, rows, outs, patches, seg, sides, plan, gain, bias, w_qkv, table):
    count, width = patches.shape
    whole = lambda *shape: pl.BlockSpec(shape, lambda i: (0,) * len(shape))
    pick = lambda k, part, size: pl.BlockSpec((1, size, width), lambda i: (k, part, 0))
    flops = 2 * count * width * sum(size for _, _, size in rows)
    args = (plan, table, seg, seg, sides, patches, gain, bias) + (w_qkv,) * len(rows)
    return pl.pallas_call(
        kernel,
        grid=(count // TILE,),
        in_specs=[
            pl.BlockSpec(memory_space=pltpu.SMEM),
            whole(*table.shape),
            whole(1, count),
            pl.BlockSpec((1, TILE), lambda i: (0, i)),
            pl.BlockSpec((1, TILE), lambda i: (0, i)),
            pl.BlockSpec((TILE, width), lambda i: (i, 0)),
            whole(width),
            whole(width),
        ]
        + [pick(*row) for row in rows],
        out_specs=[
            pl.BlockSpec(shape[:-1] + (TILE,), lambda i, n=len(shape): (0,) * (n - 1) + (i,)) for shape in outs
        ],
        out_shape=[jax.ShapeDtypeStruct(shape, BF16) for shape in outs],
        compiler_params=pltpu.CompilerParams(vmem_limit_bytes=28 << 20),
        cost_estimate=pl.CostEstimate(flops=flops, bytes_accessed=6 << 20, transcendentals=0),
        name=name,
    )(*[pltpu.with_memory_space_constraint(v, pltpu.HBM) for v in args])


def prepare_block(kv_refs, first, label, keys, values, base):
    pack = kv_refs[0].shape[1]
    rows = label_rows(label)
    extra = VAUG - HD
    ones = (lax.broadcasted_iota(jnp.int32, (extra, KB), 0) == 0).astype(F32)
    for h in range(keys.shape[0]):
        kv_ref = kv_refs[(first + h) // pack]
        place = (first + h) % pack
        block = jnp.concatenate([kv_ref[0, place, :, pl.ds(base, KB)].astype(F32), rows], axis=0)
        keys[h, pl.ds(base, KB), :] = block.astype(BF16).T
        block = jnp.concatenate([kv_ref[1, place, :, pl.ds(base, KB)].astype(F32), ones], axis=0)
        values[h, :, pl.ds(base, KB)] = block.astype(BF16)


def attend(first, q_ref, keys, values, acc, top, q_base, k_base):
    heads = keys.shape[0]
    span = pl.ds(q_base, QB)
    old = [top[first + h : first + h + 1, span] for h in range(heads)]
    scores = [
        lax.dot_general(keys[h, pl.ds(k_base, KB), :], q_ref[first + h, :, span], NN, preferred_element_type=F32)
        for h in range(heads)
    ]
    new = [jnp.maximum(old[h], jnp.max(scores[h], axis=0, keepdims=True)) for h in range(heads)]
    weights = [jnp.exp2(scores[h] - new[h]).astype(BF16) for h in range(heads)]
    parts = [
        lax.dot_general(values[h, :, pl.ds(k_base, KB)], weights[h], NN, preferred_element_type=F32)
        for h in range(heads)
    ]
    sums = [acc[h, :, span] * jnp.exp2(old[h] - new[h]) + parts[h] for h in range(heads)]
    for h in range(heads):
        acc[h, :, span] = sums[h]
        top[first + h : first + h + 1, span] = new[h]


def own_kernel(sseg_ref, seg_ref, q_ref, *refs):
    *kv_refs, acc_ref, top_ref, keys, values = refs
    count = seg_ref.shape[1]
    seg = seg_ref[...]
    for b in range(count // KB):
        prepare_block(kv_refs, 0, seg[:, b * KB : (b + 1) * KB], keys, values, b * KB)
    acc_ref[...] = jnp.zeros_like(acc_ref)
    top_ref[...] = jnp.full_like(top_ref, -BIG)

    def block(b, carry):
        q_base = pl.multiple_of(b * QB, QB)
        low = jnp.sum((seg < sseg_ref[0, q_base]).astype(jnp.int32))
        high = jnp.sum((seg <= sseg_ref[0, q_base + QB - 1]).astype(jnp.int32))

        def inner(k, c):
            attend(0, q_ref, keys, values, acc_ref, top_ref, q_base, pl.multiple_of(k * KB, KB))
            return c

        return lax.fori_loop(low // KB, (high + KB - 1) // KB, inner, carry)

    lax.fori_loop(0, count // QB, block, 0)


def own_call(seg, q, kv):
    heads, _, count = q.shape
    vmem = pl.BlockSpec(memory_space=pltpu.VMEM)
    return pl.pallas_call(
        own_kernel,
        in_specs=[pl.BlockSpec(memory_space=pltpu.SMEM)] + [vmem] * (2 + len(kv)),
        out_specs=[vmem, vmem],
        out_shape=[
            jax.ShapeDtypeStruct((heads, VAUG, count), F32),
            jax.ShapeDtypeStruct((8, count), F32),
        ],
        scratch_shapes=[pltpu.VMEM((heads, count, AUG), BF16), pltpu.VMEM((heads, VAUG, count), BF16)],
        compiler_params=pltpu.CompilerParams(vmem_limit_bytes=20 << 20),
        cost_estimate=pl.CostEstimate(flops=8 << 30, bytes_accessed=8 << 20, transcendentals=4 << 20),
        name="own_keys",
    )(seg, seg, q, *kv)


def halo_kernel(first, plan_ref, sseg_ref, q_ref, acc_in, top_in, before_ref, after_ref, out_ref, acc, top, keys, values):
    count = q_ref.shape[2]
    heads = keys.shape[0]
    acc[...] = acc_in[first : first + heads]
    top[...] = top_in[...]
    lead, trail = plan_ref[0, 0], plan_ref[0, 1]
    last = sseg_ref[0, count - 1]
    token = lax.broadcasted_iota(jnp.int32, (1, KB), 1)

    def before_block(k, carry):
        base = pl.multiple_of(k * KB, KB)
        label = jnp.where(token + base >= count - lead, 0, -1)
        prepare_block([before_ref], first, label, keys, values, base)

        def inner(b, c):
            q_base = pl.multiple_of(b * QB, QB)

            @pl.when(sseg_ref[0, q_base] == 0)
            def _():
                attend(first, q_ref, keys, values, acc, top, q_base, base)

            return c

        return lax.fori_loop(0, count // QB, inner, carry)

    lax.fori_loop((count - lead) // KB, count // KB, before_block, 0)

    def after_block(k, carry):
        base = pl.multiple_of(k * KB, KB)
        label = jnp.where(token + base < trail, last, -1)
        prepare_block([after_ref], first, label, keys, values, base)

        def inner(b, c):
            q_base = pl.multiple_of(b * QB, QB)

            @pl.when(sseg_ref[0, q_base + QB - 1] == last)
            def _():
                attend(first, q_ref, keys, values, acc, top, q_base, base)

            return c

        return lax.fori_loop(0, count // QB, inner, carry)

    lax.fori_loop(0, (trail + KB - 1) // KB, after_block, 0)
    for h in range(heads):
        out_ref[pl.ds(h * HD, HD), :] = (acc[h, :HD, :] / acc[h, HD : HD + 1, :]).astype(BF16)


def halo_call(first, plan, seg, q, acc, top, before, after):
    count = q.shape[2]
    heads = PACK
    vmem = pl.BlockSpec(memory_space=pltpu.VMEM)
    smem = pl.BlockSpec(memory_space=pltpu.SMEM)
    return pl.pallas_call(
        functools.partial(halo_kernel, first),
        in_specs=[smem, smem, vmem, vmem, vmem, vmem, vmem],
        out_specs=vmem,
        out_shape=jax.ShapeDtypeStruct((heads * HD, count), BF16),
        scratch_shapes=[
            pltpu.VMEM((heads, VAUG, count), F32),
            pltpu.VMEM(top.shape, F32),
            pltpu.VMEM((heads, count, AUG), BF16),
            pltpu.VMEM((heads, VAUG, count), BF16),
        ],
        compiler_params=pltpu.CompilerParams(vmem_limit_bytes=20 << 20),
        cost_estimate=pl.CostEstimate(flops=3 << 30, bytes_accessed=8 << 20, transcendentals=4 << 20),
        name="halo_keys",
    )(plan, seg, q, acc, top, before, after)


def gather_kernel(parts, rows, base_ref, *refs):
    out_ref = refs[-1]
    for start in range(0, out_ref.shape[0], TILE):
        span = slice(start, start + TILE)
        total = base_ref[span].astype(F32)
        for h_ref, w_ref, row in zip(refs[:parts], refs[parts : 2 * parts], rows):
            w = w_ref[row : row + h_ref.shape[0]]
            total += lax.dot_general(h_ref[:, span], w, TN, preferred_element_type=F32)
        out_ref[span] = total


def gather_call(base, heads_parts, w_parts, rows):
    vmem = pl.BlockSpec(memory_space=pltpu.VMEM)
    parts = len(heads_parts)
    flops = 2 * base.shape[0] * base.shape[1] * sum(h.shape[0] for h in heads_parts)
    return pl.pallas_call(
        functools.partial(gather_kernel, parts, rows),
        in_specs=[vmem] * (1 + 2 * parts),
        out_specs=vmem,
        out_shape=jax.ShapeDtypeStruct(base.shape, F32),
        compiler_params=pltpu.CompilerParams(vmem_limit_bytes=16 << 20),
        cost_estimate=pl.CostEstimate(flops=flops, bytes_accessed=4 << 20, transcendentals=0),
        name="output",
    )(base, *heads_parts, *w_parts)


def project_kernel(parts, starts, slot_ref, dest_ref, base_ref, *refs):
    proj, send_ref, mixed = refs[2 * parts :]
    count, width = base_ref.shape
    chunks = width // 128
    for start in range(0, count, TILE):
        span = slice(start, start + TILE)
        total = base_ref[span]
        for h_ref, w_ref, row in zip(refs[:parts], refs[parts : 2 * parts], starts):
            w = w_ref[row : row + h_ref.shape[0]]
            total += lax.dot_general(h_ref[:, span], w, TN, preferred_element_type=F32)
        for c in range(chunks):
            mixed[c, span, :] = total[:, c * 128 : (c + 1) * 128]
    rows = count // 4
    result = jnp.zeros((rows, proj.shape[1]), F32)
    for j in range(4):
        part = jnp.concatenate([mixed[c, pl.ds(j, rows, stride=4), :] for c in range(chunks)], axis=1).astype(BF16)
        result += lax.dot_general(part, proj[j * width : (j + 1) * width, :], NN, preferred_element_type=F32)
    slots = lax.broadcasted_iota(jnp.int32, (send_ref.shape[0], rows), 0)
    pick = (slots == slot_ref[...]).astype(F32)
    cols = proj.shape[1]
    send_ref[:, :cols] = lax.dot_general(
        pick.astype(BF16), result.astype(BF16), NN, preferred_element_type=F32
    ).astype(BF16)
    dest = jnp.sum(pick * dest_ref[...].astype(F32), axis=1, keepdims=True)
    send_ref[:, cols:] = jnp.broadcast_to(dest, (send_ref.shape[0], 128)).astype(BF16)


def project_call(slot, dest, base, heads_parts, w_parts, starts, w_proj, slots):
    vmem = pl.BlockSpec(memory_space=pltpu.VMEM)
    parts = len(heads_parts)
    count, width = base.shape
    cols = w_proj.shape[1]
    return pl.pallas_call(
        functools.partial(project_kernel, parts, starts),
        in_specs=[vmem] * (4 + 2 * parts),
        out_specs=vmem,
        out_shape=jax.ShapeDtypeStruct((slots, cols + 128), BF16),
        scratch_shapes=[pltpu.VMEM((width // 128, count, 128), F32)],
        compiler_params=pltpu.CompilerParams(vmem_limit_bytes=24 << 20),
        cost_estimate=pl.CostEstimate(flops=3 << 30, bytes_accessed=8 << 20, transcendentals=0),
        name="project",
    )(slot, dest, base, *heads_parts, *w_parts, w_proj)


def place_kernel(got_ref, out_ref):
    cols = out_ref.shape[1]
    dest = got_ref[:, cols:].astype(F32).astype(jnp.int32)
    dest = jnp.concatenate([dest] * (out_ref.shape[0] // 128), axis=1)
    rows = lax.broadcasted_iota(jnp.int32, dest.shape, 1)
    pick = (rows == dest).astype(F32).astype(BF16)
    out_ref[...] = lax.dot_general(pick, got_ref[:, :cols], TN, preferred_element_type=F32).astype(BF16)


def place_call(got, rows, cols):
    vmem = pl.BlockSpec(memory_space=pltpu.VMEM)
    return pl.pallas_call(
        place_kernel,
        in_specs=[vmem],
        out_specs=vmem,
        out_shape=jax.ShapeDtypeStruct((rows, cols), BF16),
        name="place",
    )(got)


def ring(axis, shift):
    size = lax.axis_size(axis)
    return [(i, (i + shift) % size) for i in range(size)]


def around(block, axis):
    half = -(-block.shape[0] // 32) * 16
    left = lax.ppermute(block, axis, ring(axis, 1))
    right = lax.ppermute(block, axis, ring(axis, -1))
    far_top = lax.ppermute(left[:half], axis, ring(axis, 1))
    far_end = lax.ppermute(right[half:], axis, ring(axis, -1))
    return left, right, far_top, far_end


def on_device(patches, segment_ids, grid_sides, split_plan, owner_dev, dest_row, ln_gain, ln_bias, w_qkv, w_out, w_proj):
    count, width = patches.shape
    local = w_qkv.shape[1]
    heads = local // HD
    rows_out = owner_dev.shape[0]
    peers = lax.axis_size("req")
    lanes = 2 * rows_out // peers
    seg = segment_ids.reshape(1, count)
    table = jnp.asarray(rope_table())
    w_left, w_right, w_top, w_end = around(w_out, "tp")
    inputs = (patches, seg, grid_sides.reshape(1, count), split_plan, ln_gain, ln_bias, w_qkv, table)
    (kv,) = qkv_call(kv_kernel, "keys_values", [(1, 0, local), (2, 0, local)], [(2, heads, HD, count)], *inputs)
    up = [(i, i + 1) for i in range(peers - 1)]
    down = [(j, i) for i, j in up]
    before = lax.ppermute(kv, "req", up)
    after = lax.ppermute(kv, "req", down)
    (q,) = qkv_call(q_kernel, "queries", [(0, 0, local)], [(heads, AUG, count)], *inputs)
    acc, top = own_call(seg, q, [kv])
    before, after, w_left, w_right, w_top, w_end = lax.optimization_barrier(
        (before, after, w_left, w_right, w_top, w_end)
    )
    pack = PACK * HD
    w_far = [w_top, w_end]
    lows = list(range(0, local, pack))
    outs, sides = [], []
    for index in range(len(lows)):
        if outs:
            acc, outs[-1] = lax.optimization_barrier((acc, outs[-1]))
        outs.append(halo_call(index * PACK, split_plan, seg, q, acc, top, before, after))
        sides.append(around(outs[-1], "tp"))
    terms = [(part, w_out, low) for part, low in zip(outs, lows)]
    base = patches
    for index, (left, right, far_top, far_end) in enumerate(sides):
        terms += [(left, w_left, lows[index]), (right, w_right, lows[index])]
        base = gather_call(base, *zip(*terms))
        terms = [(far_top, w_far[index], 0), (far_end, w_far[index], far_top.shape[0])]
    within = jnp.arange(rows_out, dtype=jnp.int32) % lanes
    slot = (owner_dev * lanes + within).reshape(1, rows_out)
    send = project_call(
        slot, dest_row.reshape(1, rows_out), base, *zip(*terms), w_proj, peers * lanes
    )
    cols = send.shape[1]
    got = lax.all_to_all(send.reshape(peers, lanes, cols), "req", split_axis=0, concat_axis=0, tiled=True)
    return place_call(got.reshape(peers * lanes, cols), rows_out, w_proj.shape[1])


def solution(mesh):
    placed = (
        P("req", None),
        P("req"),
        P("req"),
        P("req", None),
        P("req"),
        P("req"),
        P(),
        P(),
        P(None, "tp", None),
        P("tp", None),
        P(None, "tp"),
    )
    return jax.shard_map(on_device, mesh=mesh, in_specs=placed, out_specs=P("req", "tp"), check_vma=False)
```

```python
import functools

import jax
import jax.numpy as jnp
import numpy as np
from jax import lax
from jax.experimental import pallas as pl
from jax.experimental.pallas import tpu as pltpu
from jax.sharding import PartitionSpec as P

HD = 88
QUARTER = HD // 4
SIDE_MAX = 32
AUG = 128
VAUG = 96
BIG = 1e30
TILE = 256
QB = 512
KB = 256
PACK = 2
F32 = jnp.float32
BF16 = jnp.bfloat16
NT = (((1,), (1,)), ((), ()))
NN = (((1,), (0,)), ((), ()))
TN = (((0,), (0,)), ((), ()))
LOG2E = 1.4426950408889634


def rope_table():
    freq = 10000.0 ** (-np.arange(QUARTER, dtype=np.float64) / QUARTER)
    chan = np.arange(HD)
    pos = np.arange(SIDE_MAX, dtype=np.float64)
    angle = freq[chan % QUARTER][:, None] * pos[None, :]
    sign = np.where(chan % (2 * QUARTER) < QUARTER, -1.0, 1.0)[:, None]
    in_row = (chan < 2 * QUARTER)[:, None]
    halves = []
    for part in (np.cos(angle), sign * np.sin(angle)):
        halves.append(np.concatenate([np.where(in_row, part, 0.0), np.where(in_row, 0.0, part)], axis=1))
    table = np.concatenate(halves, axis=0).astype(np.float32)
    terms = []
    for _ in range(3):
        term = table.astype(jnp.bfloat16)
        terms.append(term)
        table = table - term.astype(np.float32)
    return np.concatenate(terms, axis=1)


def seg_counts(seg):
    ids = lax.broadcasted_iota(jnp.int32, (16, seg.shape[1]), 0)
    below = jnp.sum((seg < ids).astype(F32), axis=1, keepdims=True)
    return below


def label_rows(label):
    ids = lax.broadcasted_iota(jnp.int32, (AUG - HD, label.shape[1]), 0)
    return (ids == jnp.where(label < 0, 16, label)).astype(F32)


def normalised(x_ref, gain_ref, bias_ref):
    x = x_ref[...].astype(F32)
    centred = x - jnp.mean(x, axis=1, keepdims=True)
    variance = jnp.mean(centred * centred, axis=1, keepdims=True)
    scaled = centred * lax.rsqrt(variance + 1e-6) * gain_ref[...].reshape(1, -1) + bias_ref[...].reshape(1, -1)
    return scaled.astype(BF16)


def rotations(plan_ref, table_ref, seg_ref, segt_ref, side_ref):
    below = seg_counts(seg_ref[...])
    seg = segt_ref[...]
    ids = lax.broadcasted_iota(jnp.int32, (16, TILE), 0)
    start = jnp.sum(jnp.where(ids == seg, below, 0.0), axis=0, keepdims=True).astype(jnp.int32)
    token = lax.broadcasted_iota(jnp.int32, (1, TILE), 1) + pl.program_id(0) * TILE
    offset = token - start + jnp.where(seg == 0, plan_ref[0, 0], 0)
    window = lax.shift_right_logical(offset, 2)
    corner = offset & 3
    half = lax.shift_right_logical(side_ref[...], 1)
    down = jnp.floor((window.astype(F32) + 0.5) / half.astype(F32)).astype(jnp.int32)
    grid_row = 2 * down + lax.shift_right_logical(corner, 1)
    grid_col = 2 * (window - down * half) + (corner & 1)
    pos = lax.broadcasted_iota(jnp.int32, (2 * SIDE_MAX, TILE), 0)
    hot = ((pos == grid_row) | (pos == grid_col + SIDE_MAX)).astype(F32).astype(BF16)
    hot = jnp.concatenate([hot, hot, hot], axis=0)
    angles = lax.dot_general(table_ref[...], hot, NN, preferred_element_type=F32)
    cosine, sine = angles[:HD], angles[HD:]
    first = lax.broadcasted_iota(jnp.int32, (HD, TILE), 0) % (2 * QUARTER) < QUARTER

    def rotated(value):
        partner = jnp.where(first, pltpu.roll(value, HD - QUARTER, 0), pltpu.roll(value, QUARTER, 0))
        return value * cosine + partner * sine

    return rotated


def kv_kernel(plan_ref, table_ref, seg_ref, segt_ref, side_ref, x_ref, gain_ref, bias_ref, wk_ref, wv_ref, *kv_refs):
    normed = normalised(x_ref, gain_ref, bias_ref)
    rotated = rotations(plan_ref, table_ref, seg_ref, segt_ref, side_ref)
    keys = lax.dot_general(wk_ref[0], normed, NT, preferred_element_type=F32)
    values = lax.dot_general(wv_ref[0], normed, NT, preferred_element_type=F32)
    pack = kv_refs[0].shape[1]
    for h in range(pack * len(kv_refs)):
        span = slice(h * HD, (h + 1) * HD)
        kv_refs[h // pack][0, h % pack] = rotated(keys[span]).astype(BF16)
        kv_refs[h // pack][1, h % pack] = values[span].astype(BF16)


def q_kernel(plan_ref, table_ref, seg_ref, segt_ref, side_ref, x_ref, gain_ref, bias_ref, w_ref, q_ref):
    normed = normalised(x_ref, gain_ref, bias_ref)
    rotated = rotations(plan_ref, table_ref, seg_ref, segt_ref, side_ref)
    queries = lax.dot_general(w_ref[0], normed, NT, preferred_element_type=F32)
    aug = lax.broadcasted_iota(jnp.int32, (AUG - HD, TILE), 0)
    barred = jnp.where(aug == jnp.broadcast_to(segt_ref[...], aug.shape), 0.0, jnp.where(aug <= 16, -BIG, 0.0))
    for h in range(q_ref.shape[0]):
        query = rotated(queries[h * HD : (h + 1) * HD]) * (HD**-0.5 * LOG2E)
        q_ref[h] = jnp.concatenate([query, barred], axis=0).astype(BF16)


def qkv_call(kernel, name, rows, outs, patches, seg, sides, plan, gain, bias, w_qkv, table):
    count, width = patches.shape
    whole = lambda *shape: pl.BlockSpec(shape, lambda i: (0,) * len(shape))
    pick = lambda k, part, size: pl.BlockSpec((1, size, width), lambda i: (k, part, 0))
    flops = 2 * count * width * sum(size for _, _, size in rows)
    args = (plan, table, seg, seg, sides, patches, gain, bias) + (w_qkv,) * len(rows)
    return pl.pallas_call(
        kernel,
        grid=(count // TILE,),
        in_specs=[
            pl.BlockSpec(memory_space=pltpu.SMEM),
            whole(*table.shape),
            whole(1, count),
            pl.BlockSpec((1, TILE), lambda i: (0, i)),
            pl.BlockSpec((1, TILE), lambda i: (0, i)),
            pl.BlockSpec((TILE, width), lambda i: (i, 0)),
            whole(width),
            whole(width),
        ]
        + [pick(*row) for row in rows],
        out_specs=[
            pl.BlockSpec(shape[:-1] + (TILE,), lambda i, n=len(shape): (0,) * (n - 1) + (i,)) for shape in outs
        ],
        out_shape=[jax.ShapeDtypeStruct(shape, BF16) for shape in outs],
        compiler_params=pltpu.CompilerParams(vmem_limit_bytes=28 << 20),
        cost_estimate=pl.CostEstimate(flops=flops // 1, bytes_accessed=1 << 20, transcendentals=0),
        name=name,
    )(*[pltpu.with_memory_space_constraint(v, pltpu.HBM) for v in args])


def prepare_block(kv_ref, first, label, keys, values, base):
    rows = label_rows(label)
    extra = VAUG - HD
    ones = (lax.broadcasted_iota(jnp.int32, (extra, KB), 0) == 0).astype(F32)
    for h in range(keys.shape[0]):
        block = jnp.concatenate([kv_ref[0, first + h, :, pl.ds(base, KB)].astype(F32), rows], axis=0)
        keys[h, pl.ds(base, KB), :] = block.astype(BF16).T
        block = jnp.concatenate([kv_ref[1, first + h, :, pl.ds(base, KB)].astype(F32), ones], axis=0)
        values[h, :, pl.ds(base, KB)] = block.astype(BF16)


def attend(first, q_ref, keys, values, acc, top, q_base, k_base):
    heads = keys.shape[0]
    span = pl.ds(q_base, QB)
    old = [top[first + h : first + h + 1, span] for h in range(heads)]
    scores = [
        lax.dot_general(keys[h, pl.ds(k_base, KB), :], q_ref[first + h, :, span], NN, preferred_element_type=F32)
        for h in range(heads)
    ]
    new = [jnp.maximum(old[h], jnp.max(scores[h], axis=0, keepdims=True)) for h in range(heads)]
    weights = [jnp.exp2(scores[h] - new[h]).astype(BF16) for h in range(heads)]
    parts = [
        lax.dot_general(values[h, :, pl.ds(k_base, KB)], weights[h], NN, preferred_element_type=F32)
        for h in range(heads)
    ]
    sums = [acc[h, :, span] * jnp.exp2(old[h] - new[h]) + parts[h] for h in range(heads)]
    for h in range(heads):
        acc[h, :, span] = sums[h]
        top[first + h : first + h + 1, span] = new[h]


def own_kernel(sseg_ref, seg_ref, q_ref, kv_ref, acc_ref, top_ref, keys, values):
    count = seg_ref.shape[1]
    seg = seg_ref[...]
    for b in range(count // KB):
        prepare_block(kv_ref, 0, seg[:, b * KB : (b + 1) * KB], keys, values, b * KB)
    acc_ref[...] = jnp.zeros_like(acc_ref)
    top_ref[...] = jnp.full_like(top_ref, -BIG)

    def block(b, carry):
        q_base = pl.multiple_of(b * QB, QB)
        low = jnp.sum((seg < sseg_ref[0, q_base]).astype(jnp.int32))
        high = jnp.sum((seg <= sseg_ref[0, q_base + QB - 1]).astype(jnp.int32))

        def inner(k, c):
            attend(0, q_ref, keys, values, acc_ref, top_ref, q_base, pl.multiple_of(k * KB, KB))
            return c

        return lax.fori_loop(low // KB, (high + KB - 1) // KB, inner, carry)

    lax.fori_loop(0, count // QB, block, 0)


def neighbour(first, follows, plan_ref, sseg_ref, kv_ref, q_ref, keys, values, acc, top):
    count = q_ref.shape[2]
    last = sseg_ref[0, count - 1]
    begin = jnp.where(follows == 1, 0, count - plan_ref[0, 0])
    end = jnp.where(follows == 1, plan_ref[0, 1], count)
    image = jnp.where(follows == 1, last, 0)
    token = lax.broadcasted_iota(jnp.int32, (1, KB), 1)

    def block(k, carry):
        base = pl.multiple_of(k * KB, KB)
        label = jnp.where((token + base >= begin) & (token + base < end), image, -1)
        prepare_block(kv_ref, first, label, keys, values, base)

        def inner(b, c):
            q_base = pl.multiple_of(b * QB, QB)

            @pl.when(sseg_ref[0, q_base + follows * (QB - 1)] == image)
            def _():
                attend(first, q_ref, keys, values, acc, top, q_base, base)

            return c

        return lax.fori_loop(0, count // QB, inner, carry)

    lax.fori_loop(begin // KB, (end + KB - 1) // KB, block, 0)


def own_call(seg, q, kv):
    heads, _, count = q.shape
    vmem = pl.BlockSpec(memory_space=pltpu.VMEM)
    smem = pl.BlockSpec(memory_space=pltpu.SMEM)
    return pl.pallas_call(
        own_kernel,
        in_specs=[smem] + [vmem] * 3,
        out_specs=[vmem, vmem],
        out_shape=[
            jax.ShapeDtypeStruct((heads, VAUG, count), F32),
            jax.ShapeDtypeStruct((8, count), F32),
        ],
        scratch_shapes=[pltpu.VMEM((heads, count, AUG), BF16), pltpu.VMEM((heads, VAUG, count), BF16)],
        compiler_params=pltpu.CompilerParams(vmem_limit_bytes=20 << 20),
        cost_estimate=pl.CostEstimate(flops=32 << 28, bytes_accessed=1 << 20, transcendentals=0),
        name="own_keys",
    )(seg, seg, q, kv)


def near_kernel(plan_ref, sseg_ref, q_ref, acc_in, top_in, kv_ref, acc_ref, top_ref, keys, values):
    acc_ref[...] = acc_in[...]
    top_ref[...] = top_in[...]
    neighbour(0, 1 - plan_ref[0, 2], plan_ref, sseg_ref, kv_ref, q_ref, keys, values, acc_ref, top_ref)


def near_call(plan, seg, q, acc, top, kv):
    heads, _, count = q.shape
    vmem = pl.BlockSpec(memory_space=pltpu.VMEM)
    smem = pl.BlockSpec(memory_space=pltpu.SMEM)
    return pl.pallas_call(
        near_kernel,
        in_specs=[smem, smem, vmem, vmem, vmem, vmem],
        out_specs=[vmem, vmem],
        out_shape=[jax.ShapeDtypeStruct(acc.shape, F32), jax.ShapeDtypeStruct(top.shape, F32)],
        scratch_shapes=[pltpu.VMEM((heads, count, AUG), BF16), pltpu.VMEM((heads, VAUG, count), BF16)],
        compiler_params=pltpu.CompilerParams(vmem_limit_bytes=20 << 20),
        cost_estimate=pl.CostEstimate(flops=1 << 28, bytes_accessed=1 << 20, transcendentals=0),
        name="near_keys",
    )(plan, seg, q, acc, top, kv)


def far_kernel(first, plan_ref, sseg_ref, q_ref, acc_in, top_in, kv_ref, out_ref, acc, top, keys, values):
    heads = keys.shape[0]
    acc[...] = acc_in[first : first + heads]
    top[...] = top_in[...]
    neighbour(first, plan_ref[0, 2], plan_ref, sseg_ref, kv_ref, q_ref, keys, values, acc, top)
    for h in range(heads):
        out_ref[pl.ds(h * HD, HD), :] = (acc[h, :HD, :] / acc[h, HD : HD + 1, :]).astype(BF16)


def far_call(first, plan, seg, q, acc, top, kv):
    count = q.shape[2]
    vmem = pl.BlockSpec(memory_space=pltpu.VMEM)
    smem = pl.BlockSpec(memory_space=pltpu.SMEM)
    return pl.pallas_call(
        functools.partial(far_kernel, first),
        in_specs=[smem, smem, vmem, vmem, vmem, vmem],
        out_specs=vmem,
        out_shape=jax.ShapeDtypeStruct((PACK * HD, count), BF16),
        scratch_shapes=[
            pltpu.VMEM((PACK, VAUG, count), F32),
            pltpu.VMEM(top.shape, F32),
            pltpu.VMEM((PACK, count, AUG), BF16),
            pltpu.VMEM((PACK, VAUG, count), BF16),
        ],
        compiler_params=pltpu.CompilerParams(vmem_limit_bytes=20 << 20),
        cost_estimate=pl.CostEstimate(flops=12 << 28, bytes_accessed=1 << 20, transcendentals=0),
        name="far_keys",
    )(plan, seg, q, acc, top, kv)


def gather_kernel(parts, rows, base_ref, *refs):
    out_ref = refs[-1]
    for start in range(0, out_ref.shape[0], TILE):
        span = slice(start, start + TILE)
        total = base_ref[span].astype(F32)
        for h_ref, w_ref, row in zip(refs[:parts], refs[parts : 2 * parts], rows):
            w = w_ref[row : row + h_ref.shape[0]]
            total += lax.dot_general(h_ref[:, span], w, TN, preferred_element_type=F32)
        out_ref[span] = total


def gather_call(base, heads_parts, w_parts, rows):
    vmem = pl.BlockSpec(memory_space=pltpu.VMEM)
    parts = len(heads_parts)
    flops = 2 * base.shape[0] * base.shape[1] * sum(h.shape[0] for h in heads_parts)
    return pl.pallas_call(
        functools.partial(gather_kernel, parts, rows),
        in_specs=[vmem] * (1 + 2 * parts),
        out_specs=vmem,
        out_shape=jax.ShapeDtypeStruct(base.shape, F32),
        compiler_params=pltpu.CompilerParams(vmem_limit_bytes=16 << 20),
        cost_estimate=pl.CostEstimate(flops=flops // 32, bytes_accessed=1 << 16, transcendentals=0),
        name="output",
    )(base, *heads_parts, *w_parts)


def project_kernel(parts, starts, slot_ref, dest_ref, base_ref, *refs):
    proj, send_ref, mixed = refs[2 * parts :]
    count, width = base_ref.shape
    chunks = width // 128
    for start in range(0, count, TILE):
        span = slice(start, start + TILE)
        total = base_ref[span]
        for h_ref, w_ref, row in zip(refs[:parts], refs[parts : 2 * parts], starts):
            w = w_ref[row : row + h_ref.shape[0]]
            total += lax.dot_general(h_ref[:, span], w, TN, preferred_element_type=F32)
        for c in range(chunks):
            mixed[c, span, :] = total[:, c * 128 : (c + 1) * 128]
    rows = count // 4
    result = jnp.zeros((rows, proj.shape[1]), F32)
    for j in range(4):
        part = jnp.concatenate([mixed[c, pl.ds(j, rows, stride=4), :] for c in range(chunks)], axis=1).astype(BF16)
        result += lax.dot_general(part, proj[j * width : (j + 1) * width, :], NN, preferred_element_type=F32)
    slots = lax.broadcasted_iota(jnp.int32, (send_ref.shape[0], rows), 0)
    pick = (slots == slot_ref[...]).astype(F32)
    cols = proj.shape[1]
    send_ref[:, :cols] = lax.dot_general(
        pick.astype(BF16), result.astype(BF16), NN, preferred_element_type=F32
    ).astype(BF16)
    dest = jnp.sum(pick * dest_ref[...].astype(F32), axis=1, keepdims=True)
    send_ref[:, cols:] = jnp.broadcast_to(dest, (send_ref.shape[0], 128)).astype(BF16)


def project_call(slot, dest, base, heads_parts, w_parts, starts, w_proj, slots):
    vmem = pl.BlockSpec(memory_space=pltpu.VMEM)
    parts = len(heads_parts)
    count, width = base.shape
    cols = w_proj.shape[1]
    return pl.pallas_call(
        functools.partial(project_kernel, parts, starts),
        in_specs=[vmem] * (4 + 2 * parts),
        out_specs=vmem,
        out_shape=jax.ShapeDtypeStruct((slots, cols + 128), BF16),
        scratch_shapes=[pltpu.VMEM((width // 128, count, 128), F32)],
        compiler_params=pltpu.CompilerParams(vmem_limit_bytes=24 << 20),
        cost_estimate=pl.CostEstimate(flops=3 << 30, bytes_accessed=8 << 20, transcendentals=0),
        name="project",
    )(slot, dest, base, *heads_parts, *w_parts, w_proj)


def place_kernel(got_ref, out_ref):
    cols = out_ref.shape[1]
    dest = got_ref[:, cols:].astype(F32).astype(jnp.int32)
    dest = jnp.concatenate([dest] * (out_ref.shape[0] // 128), axis=1)
    rows = lax.broadcasted_iota(jnp.int32, dest.shape, 1)
    pick = (rows == dest).astype(F32).astype(BF16)
    out_ref[...] = lax.dot_general(pick, got_ref[:, :cols], TN, preferred_element_type=F32).astype(BF16)


def place_call(got, rows, cols):
    vmem = pl.BlockSpec(memory_space=pltpu.VMEM)
    return pl.pallas_call(
        place_kernel,
        in_specs=[vmem],
        out_specs=vmem,
        out_shape=jax.ShapeDtypeStruct((rows, cols), BF16),
        name="place",
    )(got)


def ring(axis, shift):
    size = lax.axis_size(axis)
    return [(i, (i + shift) % size) for i in range(size)]


def swaps(firsts):
    return [pair for i in firsts for pair in ((i, i + 1), (i + 1, i))]


def beside(block, axis):
    return lax.ppermute(block, axis, ring(axis, 1)), lax.ppermute(block, axis, ring(axis, -1))


def beyond(left, right, axis):
    half = -(-left.shape[0] // 32) * 16
    return lax.ppermute(left[:half], axis, ring(axis, 1)), lax.ppermute(right[half:], axis, ring(axis, -1))


def on_device(patches, segment_ids, grid_sides, split_plan, owner_dev, dest_row, ln_gain, ln_bias, w_qkv, w_out, w_proj):
    count, width = patches.shape
    local = w_qkv.shape[1]
    heads = local // HD
    rows_out = owner_dev.shape[0]
    peers = lax.axis_size("req")
    lanes = 2 * rows_out // peers
    seg = segment_ids.reshape(1, count)
    table = jnp.asarray(rope_table())
    w_left, w_right = beside(w_out, "tp")
    w_top, w_end = beyond(w_left, w_right, "tp")
    inputs = (patches, seg, grid_sides.reshape(1, count), split_plan, ln_gain, ln_bias, w_qkv, table)
    (kv,) = qkv_call(kv_kernel, "keys_values", [(1, 0, local), (2, 0, local)], [(2, heads, HD, count)], *inputs)
    far = lax.ppermute(kv, "req", swaps(range(1, peers - 1, 2)))
    near = lax.ppermute(kv, "req", swaps(range(0, peers - 1, 2)))
    parity = (lax.axis_index("req") % 2).astype(jnp.int32).reshape(1, 1)
    plan = jnp.concatenate([split_plan, parity], axis=1)
    (q,) = qkv_call(q_kernel, "queries", [(0, 0, local)], [(heads, AUG, count)], *inputs)
    acc, top = own_call(seg, q, kv)
    acc, top = near_call(plan, seg, q, acc, top, near)
    far, w_left, w_right, w_top, w_end = lax.optimization_barrier((far, w_left, w_right, w_top, w_end))
    pack = PACK * HD
    lows = list(range(0, local, pack))
    outs, sides = [], []
    for index in range(len(lows)):
        if outs:
            acc, outs[-1] = lax.optimization_barrier((acc, outs[-1]))
        outs.append(far_call(index * PACK, plan, seg, q, acc, top, far))
        sides.append(beside(outs[-1], "tp"))
    w_far = [w_top, w_end]
    terms = [(part, w_out, low) for part, low in zip(outs, lows)]
    base = patches
    for index, (left, right) in enumerate(sides):
        opposite = beyond(left, right, "tp")
        terms += [(left, w_left, lows[index]), (right, w_right, lows[index])]
        base = gather_call(base, *zip(*terms))
        terms = [(opposite[0], w_far[index], 0), (opposite[1], w_far[index], opposite[0].shape[0])]
    within = jnp.arange(rows_out, dtype=jnp.int32) % lanes
    slot = (owner_dev * lanes + within).reshape(1, rows_out)
    send = project_call(
        slot, dest_row.reshape(1, rows_out), base, *zip(*terms), w_proj, peers * lanes
    )
    cols = send.shape[1]
    got = lax.all_to_all(send.reshape(peers, lanes, cols), "req", split_axis=0, concat_axis=0, tiled=True)
    return place_call(got.reshape(peers * lanes, cols), rows_out, w_proj.shape[1])


def solution(mesh):
    placed = (
        P("req", None),
        P("req"),
        P("req"),
        P("req", None),
        P("req"),
        P("req"),
        P(),
        P(),
        P(None, "tp", None),
        P("tp", None),
        P(None, "tp"),
    )
    return jax.shard_map(on_device, mesh=mesh, in_specs=placed, out_specs=P("req", "tp"), check_vma=False)
```

```python
import functools

import jax
import jax.numpy as jnp
import numpy as np
from jax import lax
from jax.experimental import pallas as pl
from jax.experimental.pallas import tpu as pltpu
from jax.sharding import PartitionSpec as P

HD = 88
QUARTER = HD // 4
SIDE_MAX = 32
AUG = 128
VAUG = 96
BIG = 1e30
TILE = 256
QB = 512
KB = 256
PACK = 2
F32 = jnp.float32
BF16 = jnp.bfloat16
NT = (((1,), (1,)), ((), ()))
NN = (((1,), (0,)), ((), ()))
TN = (((0,), (0,)), ((), ()))
LOG2E = 1.4426950408889634


def rope_table():
    freq = 10000.0 ** (-np.arange(QUARTER, dtype=np.float64) / QUARTER)
    chan = np.arange(HD)
    pos = np.arange(SIDE_MAX, dtype=np.float64)
    angle = freq[chan % QUARTER][:, None] * pos[None, :]
    sign = np.where(chan % (2 * QUARTER) < QUARTER, -1.0, 1.0)[:, None]
    in_row = (chan < 2 * QUARTER)[:, None]
    halves = []
    for part in (np.cos(angle), sign * np.sin(angle)):
        halves.append(np.concatenate([np.where(in_row, part, 0.0), np.where(in_row, 0.0, part)], axis=1))
    table = np.concatenate(halves, axis=0).astype(np.float32)
    terms = []
    for _ in range(3):
        term = table.astype(jnp.bfloat16)
        terms.append(term)
        table = table - term.astype(np.float32)
    return np.concatenate(terms, axis=1)


def seg_counts(seg):
    ids = lax.broadcasted_iota(jnp.int32, (16, seg.shape[1]), 0)
    below = jnp.sum((seg < ids).astype(F32), axis=1, keepdims=True)
    return below


def label_rows(label):
    ids = lax.broadcasted_iota(jnp.int32, (AUG - HD, label.shape[1]), 0)
    return (ids == jnp.where(label < 0, 16, label)).astype(F32)


def normalised(x_ref, gain_ref, bias_ref):
    x = x_ref[...].astype(F32)
    centred = x - jnp.mean(x, axis=1, keepdims=True)
    variance = jnp.mean(centred * centred, axis=1, keepdims=True)
    scaled = centred * lax.rsqrt(variance + 1e-6) * gain_ref[...].reshape(1, -1) + bias_ref[...].reshape(1, -1)
    return scaled.astype(BF16)


def rotations(plan_ref, table_ref, seg_ref, segt_ref, side_ref):
    below = seg_counts(seg_ref[...])
    seg = segt_ref[...]
    ids = lax.broadcasted_iota(jnp.int32, (16, TILE), 0)
    start = jnp.sum(jnp.where(ids == seg, below, 0.0), axis=0, keepdims=True).astype(jnp.int32)
    token = lax.broadcasted_iota(jnp.int32, (1, TILE), 1) + pl.program_id(0) * TILE
    offset = token - start + jnp.where(seg == 0, plan_ref[0, 0], 0)
    window = lax.shift_right_logical(offset, 2)
    corner = offset & 3
    half = lax.shift_right_logical(side_ref[...], 1)
    down = jnp.floor((window.astype(F32) + 0.5) / half.astype(F32)).astype(jnp.int32)
    grid_row = 2 * down + lax.shift_right_logical(corner, 1)
    grid_col = 2 * (window - down * half) + (corner & 1)
    pos = lax.broadcasted_iota(jnp.int32, (2 * SIDE_MAX, TILE), 0)
    hot = ((pos == grid_row) | (pos == grid_col + SIDE_MAX)).astype(F32).astype(BF16)
    hot = jnp.concatenate([hot, hot, hot], axis=0)
    angles = lax.dot_general(table_ref[...], hot, NN, preferred_element_type=F32)
    cosine, sine = angles[:HD], angles[HD:]
    first = lax.broadcasted_iota(jnp.int32, (HD, TILE), 0) % (2 * QUARTER) < QUARTER

    def rotated(value):
        partner = jnp.where(first, pltpu.roll(value, HD - QUARTER, 0), pltpu.roll(value, QUARTER, 0))
        return value * cosine + partner * sine

    return rotated


def kv_kernel(plan_ref, table_ref, seg_ref, segt_ref, side_ref, x_ref, gain_ref, bias_ref, wk_ref, wv_ref, *kv_refs):
    normed = normalised(x_ref, gain_ref, bias_ref)
    rotated = rotations(plan_ref, table_ref, seg_ref, segt_ref, side_ref)
    keys = lax.dot_general(wk_ref[0], normed, NT, preferred_element_type=F32)
    values = lax.dot_general(wv_ref[0], normed, NT, preferred_element_type=F32)
    pack = kv_refs[0].shape[1]
    for h in range(pack * len(kv_refs)):
        span = slice(h * HD, (h + 1) * HD)
        kv_refs[h // pack][0, h % pack] = rotated(keys[span]).astype(BF16)
        kv_refs[h // pack][1, h % pack] = values[span].astype(BF16)


def q_kernel(plan_ref, table_ref, seg_ref, segt_ref, side_ref, x_ref, gain_ref, bias_ref, w_ref, q_ref):
    normed = normalised(x_ref, gain_ref, bias_ref)
    rotated = rotations(plan_ref, table_ref, seg_ref, segt_ref, side_ref)
    queries = lax.dot_general(w_ref[0], normed, NT, preferred_element_type=F32)
    aug = lax.broadcasted_iota(jnp.int32, (AUG - HD, TILE), 0)
    barred = jnp.where(aug == jnp.broadcast_to(segt_ref[...], aug.shape), 0.0, jnp.where(aug <= 16, -BIG, 0.0))
    for h in range(q_ref.shape[0]):
        query = rotated(queries[h * HD : (h + 1) * HD]) * (HD**-0.5 * LOG2E)
        q_ref[h] = jnp.concatenate([query, barred], axis=0).astype(BF16)


def qkv_call(kernel, name, rows, outs, patches, seg, sides, plan, gain, bias, w_qkv, table):
    count, width = patches.shape
    whole = lambda *shape: pl.BlockSpec(shape, lambda i: (0,) * len(shape))
    pick = lambda k, part, size: pl.BlockSpec((1, size, width), lambda i: (k, part, 0))
    flops = 2 * count * width * sum(size for _, _, size in rows)
    args = (plan, table, seg, seg, sides, patches, gain, bias) + (w_qkv,) * len(rows)
    return pl.pallas_call(
        kernel,
        grid=(count // TILE,),
        in_specs=[
            pl.BlockSpec(memory_space=pltpu.SMEM),
            whole(*table.shape),
            whole(1, count),
            pl.BlockSpec((1, TILE), lambda i: (0, i)),
            pl.BlockSpec((1, TILE), lambda i: (0, i)),
            pl.BlockSpec((TILE, width), lambda i: (i, 0)),
            whole(width),
            whole(width),
        ]
        + [pick(*row) for row in rows],
        out_specs=[
            pl.BlockSpec(shape[:-1] + (TILE,), lambda i, n=len(shape): (0,) * (n - 1) + (i,)) for shape in outs
        ],
        out_shape=[jax.ShapeDtypeStruct(shape, BF16) for shape in outs],
        compiler_params=pltpu.CompilerParams(vmem_limit_bytes=28 << 20),
        cost_estimate=pl.CostEstimate(flops=flops // 1, bytes_accessed=1 << 20, transcendentals=0),
        name=name,
    )(*[pltpu.with_memory_space_constraint(v, pltpu.HBM) for v in args])


def prepare_block(kv_ref, first, label, keys, values, base):
    rows = label_rows(label)
    extra = VAUG - HD
    ones = (lax.broadcasted_iota(jnp.int32, (extra, KB), 0) == 0).astype(F32)
    for h in range(keys.shape[0]):
        block = jnp.concatenate([kv_ref[0, first + h, :, pl.ds(base, KB)].astype(F32), rows], axis=0)
        keys[h, pl.ds(base, KB), :] = block.astype(BF16).T
        block = jnp.concatenate([kv_ref[1, first + h, :, pl.ds(base, KB)].astype(F32), ones], axis=0)
        values[h, :, pl.ds(base, KB)] = block.astype(BF16)


def attend(first, q_ref, keys, values, acc, top, q_base, k_base):
    heads = keys.shape[0]
    span = pl.ds(q_base, QB)
    old = [top[first + h : first + h + 1, span] for h in range(heads)]
    scores = [
        lax.dot_general(keys[h, pl.ds(k_base, KB), :], q_ref[first + h, :, span], NN, preferred_element_type=F32)
        for h in range(heads)
    ]
    new = [jnp.maximum(old[h], jnp.max(scores[h], axis=0, keepdims=True)) for h in range(heads)]
    weights = [jnp.exp2(scores[h] - new[h]).astype(BF16) for h in range(heads)]
    parts = [
        lax.dot_general(values[h, :, pl.ds(k_base, KB)], weights[h], NN, preferred_element_type=F32)
        for h in range(heads)
    ]
    sums = [acc[h, :, span] * jnp.exp2(old[h] - new[h]) + parts[h] for h in range(heads)]
    for h in range(heads):
        acc[h, :, span] = sums[h]
        top[first + h : first + h + 1, span] = new[h]


def own_kernel(sseg_ref, seg_ref, q_ref, kv_ref, acc_ref, top_ref, keys, values):
    count = seg_ref.shape[1]
    seg = seg_ref[...]
    for b in range(count // KB):
        prepare_block(kv_ref, 0, seg[:, b * KB : (b + 1) * KB], keys, values, b * KB)
    acc_ref[...] = jnp.zeros_like(acc_ref)
    top_ref[...] = jnp.full_like(top_ref, -BIG)

    def block(b, carry):
        q_base = pl.multiple_of(b * QB, QB)
        low = jnp.sum((seg < sseg_ref[0, q_base]).astype(jnp.int32))
        high = jnp.sum((seg <= sseg_ref[0, q_base + QB - 1]).astype(jnp.int32))

        def inner(k, c):
            attend(0, q_ref, keys, values, acc_ref, top_ref, q_base, pl.multiple_of(k * KB, KB))
            return c

        return lax.fori_loop(low // KB, (high + KB - 1) // KB, inner, carry)

    lax.fori_loop(0, count // QB, block, 0)


def neighbour(first, follows, plan_ref, sseg_ref, kv_ref, q_ref, keys, values, acc, top):
    count = q_ref.shape[2]
    last = sseg_ref[0, count - 1]
    begin = jnp.where(follows == 1, 0, count - plan_ref[0, 0])
    end = jnp.where(follows == 1, plan_ref[0, 1], count)
    image = jnp.where(follows == 1, last, 0)
    token = lax.broadcasted_iota(jnp.int32, (1, KB), 1)

    def block(k, carry):
        base = pl.multiple_of(k * KB, KB)
        label = jnp.where((token + base >= begin) & (token + base < end), image, -1)
        prepare_block(kv_ref, first, label, keys, values, base)

        def inner(b, c):
            q_base = pl.multiple_of(b * QB, QB)

            @pl.when(sseg_ref[0, q_base + follows * (QB - 1)] == image)
            def _():
                attend(first, q_ref, keys, values, acc, top, q_base, base)

            return c

        return lax.fori_loop(0, count // QB, inner, carry)

    lax.fori_loop(begin // KB, (end + KB - 1) // KB, block, 0)


def own_call(seg, q, kv):
    heads, _, count = q.shape
    vmem = pl.BlockSpec(memory_space=pltpu.VMEM)
    smem = pl.BlockSpec(memory_space=pltpu.SMEM)
    return pl.pallas_call(
        own_kernel,
        in_specs=[smem] + [vmem] * 3,
        out_specs=[vmem, vmem],
        out_shape=[
            jax.ShapeDtypeStruct((heads, VAUG, count), F32),
            jax.ShapeDtypeStruct((8, count), F32),
        ],
        scratch_shapes=[pltpu.VMEM((heads, count, AUG), BF16), pltpu.VMEM((heads, VAUG, count), BF16)],
        compiler_params=pltpu.CompilerParams(vmem_limit_bytes=20 << 20),
        cost_estimate=pl.CostEstimate(flops=64 << 28, bytes_accessed=1 << 20, transcendentals=0),
        name="own_keys",
    )(seg, seg, q, kv)


def near_kernel(plan_ref, sseg_ref, q_ref, acc_in, top_in, kv_ref, acc_ref, top_ref, keys, values):
    acc_ref[...] = acc_in[...]
    top_ref[...] = top_in[...]
    neighbour(0, 1 - plan_ref[0, 2], plan_ref, sseg_ref, kv_ref, q_ref, keys, values, acc_ref, top_ref)


def near_call(plan, seg, q, acc, top, kv):
    heads, _, count = q.shape
    vmem = pl.BlockSpec(memory_space=pltpu.VMEM)
    smem = pl.BlockSpec(memory_space=pltpu.SMEM)
    return pl.pallas_call(
        near_kernel,
        in_specs=[smem, smem, vmem, vmem, vmem, vmem],
        out_specs=[vmem, vmem],
        out_shape=[jax.ShapeDtypeStruct(acc.shape, F32), jax.ShapeDtypeStruct(top.shape, F32)],
        scratch_shapes=[pltpu.VMEM((heads, count, AUG), BF16), pltpu.VMEM((heads, VAUG, count), BF16)],
        compiler_params=pltpu.CompilerParams(vmem_limit_bytes=20 << 20),
        cost_estimate=pl.CostEstimate(flops=1 << 28, bytes_accessed=1 << 20, transcendentals=0),
        name="near_keys",
    )(plan, seg, q, acc, top, kv)


def far_kernel(first, plan_ref, sseg_ref, q_ref, acc_in, top_in, kv_ref, out_ref, acc, top, keys, values):
    heads = keys.shape[0]
    acc[...] = acc_in[first : first + heads]
    top[...] = top_in[...]
    neighbour(first, plan_ref[0, 2], plan_ref, sseg_ref, kv_ref, q_ref, keys, values, acc, top)
    for h in range(heads):
        out_ref[pl.ds(h * HD, HD), :] = (acc[h, :HD, :] / acc[h, HD : HD + 1, :]).astype(BF16)


def far_call(first, plan, seg, q, acc, top, kv):
    count = q.shape[2]
    vmem = pl.BlockSpec(memory_space=pltpu.VMEM)
    smem = pl.BlockSpec(memory_space=pltpu.SMEM)
    return pl.pallas_call(
        functools.partial(far_kernel, first),
        in_specs=[smem, smem, vmem, vmem, vmem, vmem],
        out_specs=vmem,
        out_shape=jax.ShapeDtypeStruct((PACK * HD, count), BF16),
        scratch_shapes=[
            pltpu.VMEM((PACK, VAUG, count), F32),
            pltpu.VMEM(top.shape, F32),
            pltpu.VMEM((PACK, count, AUG), BF16),
            pltpu.VMEM((PACK, VAUG, count), BF16),
        ],
        compiler_params=pltpu.CompilerParams(vmem_limit_bytes=20 << 20),
        cost_estimate=pl.CostEstimate(flops=12 << 28, bytes_accessed=1 << 20, transcendentals=0),
        name="far_keys",
    )(plan, seg, q, acc, top, kv)


def gather_kernel(parts, rows, base_ref, *refs):
    out_ref = refs[-1]
    for start in range(0, out_ref.shape[0], TILE):
        span = slice(start, start + TILE)
        total = base_ref[span].astype(F32)
        for h_ref, w_ref, row in zip(refs[:parts], refs[parts : 2 * parts], rows):
            w = w_ref[row : row + h_ref.shape[0]]
            total += lax.dot_general(h_ref[:, span], w, TN, preferred_element_type=F32)
        out_ref[span] = total


def gather_call(base, heads_parts, w_parts, rows):
    vmem = pl.BlockSpec(memory_space=pltpu.VMEM)
    parts = len(heads_parts)
    flops = 2 * base.shape[0] * base.shape[1] * sum(h.shape[0] for h in heads_parts)
    return pl.pallas_call(
        functools.partial(gather_kernel, parts, rows),
        in_specs=[vmem] * (1 + 2 * parts),
        out_specs=vmem,
        out_shape=jax.ShapeDtypeStruct(base.shape, F32),
        compiler_params=pltpu.CompilerParams(vmem_limit_bytes=16 << 20),
        cost_estimate=pl.CostEstimate(flops=flops // 8, bytes_accessed=1 << 16, transcendentals=0),
        name="output",
    )(base, *heads_parts, *w_parts)


def project_kernel(parts, starts, slot_ref, dest_ref, base_ref, *refs):
    proj, send_ref, mixed = refs[2 * parts :]
    count, width = base_ref.shape
    chunks = width // 128
    for start in range(0, count, TILE):
        span = slice(start, start + TILE)
        total = base_ref[span]
        for h_ref, w_ref, row in zip(refs[:parts], refs[parts : 2 * parts], starts):
            w = w_ref[row : row + h_ref.shape[0]]
            total += lax.dot_general(h_ref[:, span], w, TN, preferred_element_type=F32)
        for c in range(chunks):
            mixed[c, span, :] = total[:, c * 128 : (c + 1) * 128]
    rows = count // 4
    result = jnp.zeros((rows, proj.shape[1]), F32)
    for j in range(4):
        part = jnp.concatenate([mixed[c, pl.ds(j, rows, stride=4), :] for c in range(chunks)], axis=1).astype(BF16)
        result += lax.dot_general(part, proj[j * width : (j + 1) * width, :], NN, preferred_element_type=F32)
    slots = lax.broadcasted_iota(jnp.int32, (send_ref.shape[0], rows), 0)
    pick = (slots == slot_ref[...]).astype(F32)
    cols = proj.shape[1]
    send_ref[:, :cols] = lax.dot_general(
        pick.astype(BF16), result.astype(BF16), NN, preferred_element_type=F32
    ).astype(BF16)
    dest = jnp.sum(pick * dest_ref[...].astype(F32), axis=1, keepdims=True)
    send_ref[:, cols:] = jnp.broadcast_to(dest, (send_ref.shape[0], 128)).astype(BF16)


def project_call(slot, dest, base, heads_parts, w_parts, starts, w_proj, slots):
    vmem = pl.BlockSpec(memory_space=pltpu.VMEM)
    parts = len(heads_parts)
    count, width = base.shape
    cols = w_proj.shape[1]
    return pl.pallas_call(
        functools.partial(project_kernel, parts, starts),
        in_specs=[vmem] * (4 + 2 * parts),
        out_specs=vmem,
        out_shape=jax.ShapeDtypeStruct((slots, cols + 128), BF16),
        scratch_shapes=[pltpu.VMEM((width // 128, count, 128), F32)],
        compiler_params=pltpu.CompilerParams(vmem_limit_bytes=24 << 20),
        cost_estimate=pl.CostEstimate(flops=3 << 30, bytes_accessed=8 << 20, transcendentals=0),
        name="project",
    )(slot, dest, base, *heads_parts, *w_parts, w_proj)


def place_kernel(got_ref, out_ref):
    cols = out_ref.shape[1]
    dest = got_ref[:, cols:].astype(F32).astype(jnp.int32)
    dest = jnp.concatenate([dest] * (out_ref.shape[0] // 128), axis=1)
    rows = lax.broadcasted_iota(jnp.int32, dest.shape, 1)
    pick = (rows == dest).astype(F32).astype(BF16)
    out_ref[...] = lax.dot_general(pick, got_ref[:, :cols], TN, preferred_element_type=F32).astype(BF16)


def place_call(got, rows, cols):
    vmem = pl.BlockSpec(memory_space=pltpu.VMEM)
    return pl.pallas_call(
        place_kernel,
        in_specs=[vmem],
        out_specs=vmem,
        out_shape=jax.ShapeDtypeStruct((rows, cols), BF16),
        name="place",
    )(got)


def ring(axis, shift):
    size = lax.axis_size(axis)
    return [(i, (i + shift) % size) for i in range(size)]


def swaps(firsts):
    return [pair for i in firsts for pair in ((i, i + 1), (i + 1, i))]


def beside(block, axis):
    return lax.ppermute(block, axis, ring(axis, 1)), lax.ppermute(block, axis, ring(axis, -1))


def beyond(left, right, axis):
    half = -(-left.shape[0] // 32) * 16
    return lax.ppermute(left[:half], axis, ring(axis, 1)), lax.ppermute(right[half:], axis, ring(axis, -1))


def on_device(patches, segment_ids, grid_sides, split_plan, owner_dev, dest_row, ln_gain, ln_bias, w_qkv, w_out, w_proj):
    count, width = patches.shape
    local = w_qkv.shape[1]
    heads = local // HD
    rows_out = owner_dev.shape[0]
    peers = lax.axis_size("req")
    lanes = 2 * rows_out // peers
    seg = segment_ids.reshape(1, count)
    table = jnp.asarray(rope_table())
    w_left, w_right = beside(w_out, "tp")
    inputs = (patches, seg, grid_sides.reshape(1, count), split_plan, ln_gain, ln_bias, w_qkv, table)
    (kv,) = qkv_call(kv_kernel, "keys_values", [(1, 0, local), (2, 0, local)], [(2, heads, HD, count)], *inputs)
    far = lax.ppermute(kv, "req", swaps(range(1, peers - 1, 2)))
    near = lax.ppermute(kv, "req", swaps(range(0, peers - 1, 2)))
    parity = (lax.axis_index("req") % 2).astype(jnp.int32).reshape(1, 1)
    plan = jnp.concatenate([split_plan, parity], axis=1)
    (q,) = qkv_call(q_kernel, "queries", [(0, 0, local)], [(heads, AUG, count)], *inputs)
    acc, top = own_call(seg, q, kv)
    acc, w_left, w_right = lax.optimization_barrier((acc, w_left, w_right))
    w_top, w_end = beyond(w_left, w_right, "tp")
    acc, top = near_call(plan, seg, q, acc, top, near)
    pack = PACK * HD
    lows = list(range(0, local, pack))
    outs, sides = [], []
    for index in range(len(lows)):
        if outs:
            acc, outs[-1], w_top, w_end = lax.optimization_barrier((acc, outs[-1], w_top, w_end))
        outs.append(far_call(index * PACK, plan, seg, q, acc, top, far))
        sides.append(beside(outs[-1], "tp"))
    w_far = [w_top, w_end]
    terms = [(part, w_out, low) for part, low in zip(outs, lows)]
    base = patches
    for index, (left, right) in enumerate(sides):
        if index:
            base, left, right = lax.optimization_barrier((base, left, right))
        opposite = beyond(left, right, "tp")
        terms += [(left, w_left, lows[index]), (right, w_right, lows[index])]
        base = gather_call(base, *zip(*terms))
        terms = [(opposite[0], w_far[index], 0), (opposite[1], w_far[index], opposite[0].shape[0])]
    within = jnp.arange(rows_out, dtype=jnp.int32) % lanes
    slot = (owner_dev * lanes + within).reshape(1, rows_out)
    send = project_call(
        slot, dest_row.reshape(1, rows_out), base, *zip(*terms), w_proj, peers * lanes
    )
    cols = send.shape[1]
    got = lax.all_to_all(send.reshape(peers, lanes, cols), "req", split_axis=0, concat_axis=0, tiled=True)
    return place_call(got.reshape(peers * lanes, cols), rows_out, w_proj.shape[1])


def solution(mesh):
    placed = (
        P("req", None),
        P("req"),
        P("req"),
        P("req", None),
        P("req"),
        P("req"),
        P(),
        P(),
        P(None, "tp", None),
        P("tp", None),
        P(None, "tp"),
    )
    return jax.shard_map(on_device, mesh=mesh, in_specs=placed, out_specs=P("req", "tp"), check_vma=False)
```

```python
import functools

import jax
import jax.numpy as jnp
import numpy as np
from jax import lax
from jax.experimental import pallas as pl
from jax.experimental.pallas import tpu as pltpu
from jax.sharding import PartitionSpec as P

HD = 88
QUARTER = HD // 4
SIDE_MAX = 32
AUG = 128
VAUG = 96
BIG = 1e30
TILE = 256
QB = 512
KB = 256
PACK = 2
F32 = jnp.float32
BF16 = jnp.bfloat16
NT = (((1,), (1,)), ((), ()))
NN = (((1,), (0,)), ((), ()))
TN = (((0,), (0,)), ((), ()))
LOG2E = 1.4426950408889634


def rope_table():
    freq = 10000.0 ** (-np.arange(QUARTER, dtype=np.float64) / QUARTER)
    chan = np.arange(HD)
    pos = np.arange(SIDE_MAX, dtype=np.float64)
    angle = freq[chan % QUARTER][:, None] * pos[None, :]
    sign = np.where(chan % (2 * QUARTER) < QUARTER, -1.0, 1.0)[:, None]
    in_row = (chan < 2 * QUARTER)[:, None]
    halves = []
    for part in (np.cos(angle), sign * np.sin(angle)):
        halves.append(np.concatenate([np.where(in_row, part, 0.0), np.where(in_row, 0.0, part)], axis=1))
    table = np.concatenate(halves, axis=0).astype(np.float32)
    terms = []
    for _ in range(3):
        term = table.astype(jnp.bfloat16)
        terms.append(term)
        table = table - term.astype(np.float32)
    return np.concatenate(terms, axis=1)


def seg_counts(seg):
    ids = lax.broadcasted_iota(jnp.int32, (16, seg.shape[1]), 0)
    below = jnp.sum((seg < ids).astype(F32), axis=1, keepdims=True)
    return below


def label_rows(label):
    ids = lax.broadcasted_iota(jnp.int32, (AUG - HD, label.shape[1]), 0)
    return (ids == jnp.where(label < 0, 16, label)).astype(F32)


def normalised(x_ref, gain_ref, bias_ref):
    x = x_ref[...].astype(F32)
    centred = x - jnp.mean(x, axis=1, keepdims=True)
    variance = jnp.mean(centred * centred, axis=1, keepdims=True)
    scaled = centred * lax.rsqrt(variance + 1e-6) * gain_ref[...].reshape(1, -1) + bias_ref[...].reshape(1, -1)
    return scaled.astype(BF16)


def rotations(plan_ref, table_ref, seg_ref, segt_ref, side_ref):
    below = seg_counts(seg_ref[...])
    seg = segt_ref[...]
    ids = lax.broadcasted_iota(jnp.int32, (16, TILE), 0)
    start = jnp.sum(jnp.where(ids == seg, below, 0.0), axis=0, keepdims=True).astype(jnp.int32)
    token = lax.broadcasted_iota(jnp.int32, (1, TILE), 1) + pl.program_id(0) * TILE
    offset = token - start + jnp.where(seg == 0, plan_ref[0, 0], 0)
    window = lax.shift_right_logical(offset, 2)
    corner = offset & 3
    half = lax.shift_right_logical(side_ref[...], 1)
    down = jnp.floor((window.astype(F32) + 0.5) / half.astype(F32)).astype(jnp.int32)
    grid_row = 2 * down + lax.shift_right_logical(corner, 1)
    grid_col = 2 * (window - down * half) + (corner & 1)
    pos = lax.broadcasted_iota(jnp.int32, (2 * SIDE_MAX, TILE), 0)
    hot = ((pos == grid_row) | (pos == grid_col + SIDE_MAX)).astype(F32).astype(BF16)
    hot = jnp.concatenate([hot, hot, hot], axis=0)
    angles = lax.dot_general(table_ref[...], hot, NN, preferred_element_type=F32)
    cosine, sine = angles[:HD], angles[HD:]
    first = lax.broadcasted_iota(jnp.int32, (HD, TILE), 0) % (2 * QUARTER) < QUARTER

    def rotated(value):
        partner = jnp.where(first, pltpu.roll(value, HD - QUARTER, 0), pltpu.roll(value, QUARTER, 0))
        return value * cosine + partner * sine

    return rotated


def kv_kernel(plan_ref, table_ref, seg_ref, segt_ref, side_ref, x_ref, gain_ref, bias_ref, wk_ref, wv_ref, *kv_refs):
    normed = normalised(x_ref, gain_ref, bias_ref)
    rotated = rotations(plan_ref, table_ref, seg_ref, segt_ref, side_ref)
    keys = lax.dot_general(wk_ref[0], normed, NT, preferred_element_type=F32)
    values = lax.dot_general(wv_ref[0], normed, NT, preferred_element_type=F32)
    pack = kv_refs[0].shape[1]
    for h in range(pack * len(kv_refs)):
        span = slice(h * HD, (h + 1) * HD)
        kv_refs[h // pack][0, h % pack] = rotated(keys[span]).astype(BF16)
        kv_refs[h // pack][1, h % pack] = values[span].astype(BF16)


def q_kernel(plan_ref, table_ref, seg_ref, segt_ref, side_ref, x_ref, gain_ref, bias_ref, w_ref, q_ref):
    normed = normalised(x_ref, gain_ref, bias_ref)
    rotated = rotations(plan_ref, table_ref, seg_ref, segt_ref, side_ref)
    queries = lax.dot_general(w_ref[0], normed, NT, preferred_element_type=F32)
    aug = lax.broadcasted_iota(jnp.int32, (AUG - HD, TILE), 0)
    barred = jnp.where(aug == jnp.broadcast_to(segt_ref[...], aug.shape), 0.0, jnp.where(aug <= 16, -BIG, 0.0))
    for h in range(q_ref.shape[0]):
        query = rotated(queries[h * HD : (h + 1) * HD]) * (HD**-0.5 * LOG2E)
        q_ref[h] = jnp.concatenate([query, barred], axis=0).astype(BF16)


def qkv_call(kernel, name, rows, outs, patches, seg, sides, plan, gain, bias, w_qkv, table):
    count, width = patches.shape
    whole = lambda *shape: pl.BlockSpec(shape, lambda i: (0,) * len(shape))
    pick = lambda k, part, size: pl.BlockSpec((1, size, width), lambda i: (k, part, 0))
    flops = 2 * count * width * sum(size for _, _, size in rows)
    args = (plan, table, seg, seg, sides, patches, gain, bias) + (w_qkv,) * len(rows)
    return pl.pallas_call(
        kernel,
        grid=(count // TILE,),
        in_specs=[
            pl.BlockSpec(memory_space=pltpu.SMEM),
            whole(*table.shape),
            whole(1, count),
            pl.BlockSpec((1, TILE), lambda i: (0, i)),
            pl.BlockSpec((1, TILE), lambda i: (0, i)),
            pl.BlockSpec((TILE, width), lambda i: (i, 0)),
            whole(width),
            whole(width),
        ]
        + [pick(*row) for row in rows],
        out_specs=[
            pl.BlockSpec(shape[:-1] + (TILE,), lambda i, n=len(shape): (0,) * (n - 1) + (i,)) for shape in outs
        ],
        out_shape=[jax.ShapeDtypeStruct(shape, BF16) for shape in outs],
        compiler_params=pltpu.CompilerParams(vmem_limit_bytes=12 << 20),
        cost_estimate=pl.CostEstimate(flops=flops // 1, bytes_accessed=1 << 20, transcendentals=0),
        name=name,
    )(*[pltpu.with_memory_space_constraint(v, pltpu.HBM) for v in args])


def prepare_block(kv_ref, first, label, keys, values, base):
    rows = label_rows(label)
    extra = VAUG - HD
    ones = (lax.broadcasted_iota(jnp.int32, (extra, KB), 0) == 0).astype(F32)
    for h in range(keys.shape[0]):
        block = jnp.concatenate([kv_ref[0, first + h, :, pl.ds(base, KB)].astype(F32), rows], axis=0)
        keys[h, pl.ds(base, KB), :] = block.astype(BF16).T
        block = jnp.concatenate([kv_ref[1, first + h, :, pl.ds(base, KB)].astype(F32), ones], axis=0)
        values[h, :, pl.ds(base, KB)] = block.astype(BF16)


def attend(first, q_ref, keys, values, acc, top, q_base, k_base):
    heads = keys.shape[0]
    span = pl.ds(q_base, QB)
    old = [top[first + h : first + h + 1, span] for h in range(heads)]
    scores = [
        lax.dot_general(keys[h, pl.ds(k_base, KB), :], q_ref[first + h, :, span], NN, preferred_element_type=F32)
        for h in range(heads)
    ]
    new = [jnp.maximum(old[h], jnp.max(scores[h], axis=0, keepdims=True)) for h in range(heads)]
    weights = [jnp.exp2(scores[h] - new[h]).astype(BF16) for h in range(heads)]
    parts = [
        lax.dot_general(values[h, :, pl.ds(k_base, KB)], weights[h], NN, preferred_element_type=F32)
        for h in range(heads)
    ]
    sums = [acc[h, :, span] * jnp.exp2(old[h] - new[h]) + parts[h] for h in range(heads)]
    for h in range(heads):
        acc[h, :, span] = sums[h]
        top[first + h : first + h + 1, span] = new[h]


def own_kernel(sseg_ref, seg_ref, q_ref, kv_ref, acc_ref, top_ref, keys, values):
    count = seg_ref.shape[1]
    seg = seg_ref[...]
    for b in range(count // KB):
        prepare_block(kv_ref, 0, seg[:, b * KB : (b + 1) * KB], keys, values, b * KB)
    acc_ref[...] = jnp.zeros_like(acc_ref)
    top_ref[...] = jnp.full_like(top_ref, -BIG)

    def block(b, carry):
        q_base = pl.multiple_of(b * QB, QB)
        low = jnp.sum((seg < sseg_ref[0, q_base]).astype(jnp.int32))
        high = jnp.sum((seg <= sseg_ref[0, q_base + QB - 1]).astype(jnp.int32))

        def inner(k, c):
            attend(0, q_ref, keys, values, acc_ref, top_ref, q_base, pl.multiple_of(k * KB, KB))
            return c

        return lax.fori_loop(low // KB, (high + KB - 1) // KB, inner, carry)

    lax.fori_loop(0, count // QB, block, 0)


def neighbour(first, follows, plan_ref, sseg_ref, kv_ref, q_ref, keys, values, acc, top):
    count = q_ref.shape[2]
    last = sseg_ref[0, count - 1]
    begin = jnp.where(follows == 1, 0, count - plan_ref[0, 0])
    end = jnp.where(follows == 1, plan_ref[0, 1], count)
    image = jnp.where(follows == 1, last, 0)
    token = lax.broadcasted_iota(jnp.int32, (1, KB), 1)

    def block(k, carry):
        base = pl.multiple_of(k * KB, KB)
        label = jnp.where((token + base >= begin) & (token + base < end), image, -1)
        prepare_block(kv_ref, first, label, keys, values, base)

        def inner(b, c):
            q_base = pl.multiple_of(b * QB, QB)

            @pl.when(sseg_ref[0, q_base + follows * (QB - 1)] == image)
            def _():
                attend(first, q_ref, keys, values, acc, top, q_base, base)

            return c

        return lax.fori_loop(0, count // QB, inner, carry)

    lax.fori_loop(begin // KB, (end + KB - 1) // KB, block, 0)


def own_call(seg, q, kv):
    heads, _, count = q.shape
    vmem = pl.BlockSpec(memory_space=pltpu.VMEM)
    smem = pl.BlockSpec(memory_space=pltpu.SMEM)
    return pl.pallas_call(
        own_kernel,
        in_specs=[smem] + [vmem] * 3,
        out_specs=[vmem, vmem],
        out_shape=[
            jax.ShapeDtypeStruct((heads, VAUG, count), F32),
            jax.ShapeDtypeStruct((8, count), F32),
        ],
        scratch_shapes=[pltpu.VMEM((heads, count, AUG), BF16), pltpu.VMEM((heads, VAUG, count), BF16)],
        compiler_params=pltpu.CompilerParams(vmem_limit_bytes=10 << 20),
        cost_estimate=pl.CostEstimate(flops=64 << 28, bytes_accessed=1 << 20, transcendentals=0),
        name="own_keys",
    )(seg, seg, q, kv)


def near_kernel(plan_ref, sseg_ref, q_ref, acc_in, top_in, kv_ref, acc_ref, top_ref, keys, values):
    acc_ref[...] = acc_in[...]
    top_ref[...] = top_in[...]
    neighbour(0, 1 - plan_ref[0, 2], plan_ref, sseg_ref, kv_ref, q_ref, keys, values, acc_ref, top_ref)


def near_call(plan, seg, q, acc, top, kv):
    heads, _, count = q.shape
    vmem = pl.BlockSpec(memory_space=pltpu.VMEM)
    smem = pl.BlockSpec(memory_space=pltpu.SMEM)
    return pl.pallas_call(
        near_kernel,
        in_specs=[smem, smem, vmem, vmem, vmem, vmem],
        out_specs=[vmem, vmem],
        out_shape=[jax.ShapeDtypeStruct(acc.shape, F32), jax.ShapeDtypeStruct(top.shape, F32)],
        scratch_shapes=[pltpu.VMEM((heads, count, AUG), BF16), pltpu.VMEM((heads, VAUG, count), BF16)],
        compiler_params=pltpu.CompilerParams(vmem_limit_bytes=10 << 20),
        cost_estimate=pl.CostEstimate(flops=1 << 28, bytes_accessed=1 << 20, transcendentals=0),
        name="near_keys",
    )(plan, seg, q, acc, top, kv)


def far_kernel(first, plan_ref, sseg_ref, q_ref, acc_in, top_in, kv_ref, out_ref, acc, top, keys, values):
    heads = keys.shape[0]
    acc[...] = acc_in[first : first + heads]
    top[...] = top_in[...]
    neighbour(first, plan_ref[0, 2], plan_ref, sseg_ref, kv_ref, q_ref, keys, values, acc, top)
    for h in range(heads):
        out_ref[pl.ds(h * HD, HD), :] = (acc[h, :HD, :] * (1.0 / acc[h, HD : HD + 1, :])).astype(BF16)


def far_call(first, plan, seg, q, acc, top, kv):
    count = q.shape[2]
    vmem = pl.BlockSpec(memory_space=pltpu.VMEM)
    smem = pl.BlockSpec(memory_space=pltpu.SMEM)
    return pl.pallas_call(
        functools.partial(far_kernel, first),
        in_specs=[smem, smem, vmem, vmem, vmem, vmem],
        out_specs=vmem,
        out_shape=jax.ShapeDtypeStruct((PACK * HD, count), BF16),
        scratch_shapes=[
            pltpu.VMEM((PACK, VAUG, count), F32),
            pltpu.VMEM(top.shape, F32),
            pltpu.VMEM((PACK, count, AUG), BF16),
            pltpu.VMEM((PACK, VAUG, count), BF16),
        ],
        compiler_params=pltpu.CompilerParams(vmem_limit_bytes=10 << 20),
        cost_estimate=pl.CostEstimate(flops=12 << 28, bytes_accessed=1 << 20, transcendentals=0),
        name="far_keys",
    )(plan, seg, q, acc, top, kv)


def gather_kernel(parts, rows, base_ref, *refs):
    out_ref = refs[-1]
    for start in range(0, out_ref.shape[0], TILE):
        span = slice(start, start + TILE)
        total = base_ref[span].astype(F32)
        for h_ref, w_ref, row in zip(refs[:parts], refs[parts : 2 * parts], rows):
            w = w_ref[row : row + h_ref.shape[0]]
            total += lax.dot_general(h_ref[:, span], w, TN, preferred_element_type=F32)
        out_ref[span] = total


def gather_call(base, heads_parts, w_parts, rows):
    vmem = pl.BlockSpec(memory_space=pltpu.VMEM)
    parts = len(heads_parts)
    flops = 2 * base.shape[0] * base.shape[1] * sum(h.shape[0] for h in heads_parts)
    return pl.pallas_call(
        functools.partial(gather_kernel, parts, rows),
        in_specs=[vmem] * (1 + 2 * parts),
        out_specs=vmem,
        out_shape=jax.ShapeDtypeStruct(base.shape, F32),
        compiler_params=pltpu.CompilerParams(vmem_limit_bytes=12 << 20),
        cost_estimate=pl.CostEstimate(flops=flops // 8, bytes_accessed=1 << 16, transcendentals=0),
        name="output",
    )(base, *heads_parts, *w_parts)


def project_kernel(parts, starts, slot_ref, dest_ref, base_ref, *refs):
    proj, send_ref, mixed = refs[2 * parts :]
    count, width = base_ref.shape
    chunks = width // 128
    for start in range(0, count, TILE):
        span = slice(start, start + TILE)
        total = base_ref[span]
        for h_ref, w_ref, row in zip(refs[:parts], refs[parts : 2 * parts], starts):
            w = w_ref[row : row + h_ref.shape[0]]
            total += lax.dot_general(h_ref[:, span], w, TN, preferred_element_type=F32)
        for c in range(chunks):
            mixed[c, span, :] = total[:, c * 128 : (c + 1) * 128]
    rows = count // 4
    result = jnp.zeros((rows, proj.shape[1]), F32)
    for j in range(4):
        part = jnp.concatenate([mixed[c, pl.ds(j, rows, stride=4), :] for c in range(chunks)], axis=1).astype(BF16)
        result += lax.dot_general(part, proj[j * width : (j + 1) * width, :], NN, preferred_element_type=F32)
    slots = lax.broadcasted_iota(jnp.int32, (send_ref.shape[0], rows), 0)
    pick = (slots == slot_ref[...]).astype(F32)
    cols = proj.shape[1]
    send_ref[:, :cols] = lax.dot_general(
        pick.astype(BF16), result.astype(BF16), NN, preferred_element_type=F32
    ).astype(BF16)
    dest = jnp.sum(pick * dest_ref[...].astype(F32), axis=1, keepdims=True)
    send_ref[:, cols:] = jnp.broadcast_to(dest, (send_ref.shape[0], 128)).astype(BF16)


def project_call(slot, dest, base, heads_parts, w_parts, starts, w_proj, slots):
    vmem = pl.BlockSpec(memory_space=pltpu.VMEM)
    parts = len(heads_parts)
    count, width = base.shape
    cols = w_proj.shape[1]
    return pl.pallas_call(
        functools.partial(project_kernel, parts, starts),
        in_specs=[vmem] * (4 + 2 * parts),
        out_specs=vmem,
        out_shape=jax.ShapeDtypeStruct((slots, cols + 128), BF16),
        scratch_shapes=[pltpu.VMEM((width // 128, count, 128), F32)],
        compiler_params=pltpu.CompilerParams(vmem_limit_bytes=20 << 20),
        cost_estimate=pl.CostEstimate(flops=3 << 30, bytes_accessed=8 << 20, transcendentals=0),
        name="project",
    )(slot, dest, base, *heads_parts, *w_parts, w_proj)


def place_kernel(got_ref, out_ref):
    cols = out_ref.shape[1]
    dest = got_ref[:, cols:].astype(F32).astype(jnp.int32)
    dest = jnp.concatenate([dest] * (out_ref.shape[0] // 128), axis=1)
    rows = lax.broadcasted_iota(jnp.int32, dest.shape, 1)
    pick = (rows == dest).astype(F32).astype(BF16)
    out_ref[...] = lax.dot_general(pick, got_ref[:, :cols], TN, preferred_element_type=F32).astype(BF16)


def place_call(got, rows, cols):
    vmem = pl.BlockSpec(memory_space=pltpu.VMEM)
    return pl.pallas_call(
        place_kernel,
        in_specs=[vmem],
        out_specs=vmem,
        out_shape=jax.ShapeDtypeStruct((rows, cols), BF16),
        name="place",
    )(got)


def ring(axis, shift):
    size = lax.axis_size(axis)
    return [(i, (i + shift) % size) for i in range(size)]


def swaps(firsts):
    return [pair for i in firsts for pair in ((i, i + 1), (i + 1, i))]


def beside(block, axis):
    return lax.ppermute(block, axis, ring(axis, 1)), lax.ppermute(block, axis, ring(axis, -1))


def beyond(left, right, axis):
    half = -(-left.shape[0] // 32) * 16
    return lax.ppermute(left[:half], axis, ring(axis, 1)), lax.ppermute(right[half:], axis, ring(axis, -1))


def on_device(patches, segment_ids, grid_sides, split_plan, owner_dev, dest_row, ln_gain, ln_bias, w_qkv, w_out, w_proj):
    count, width = patches.shape
    local = w_qkv.shape[1]
    heads = local // HD
    rows_out = owner_dev.shape[0]
    peers = lax.axis_size("req")
    lanes = 2 * rows_out // peers
    seg = segment_ids.reshape(1, count)
    table = jnp.asarray(rope_table())
    w_left, w_right = beside(w_out, "tp")
    inputs = (patches, seg, grid_sides.reshape(1, count), split_plan, ln_gain, ln_bias, w_qkv, table)
    (kv,) = qkv_call(kv_kernel, "keys_values", [(1, 0, local), (2, 0, local)], [(2, heads, HD, count)], *inputs)
    far = lax.ppermute(kv, "req", swaps(range(1, peers - 1, 2)))
    near = lax.ppermute(kv, "req", swaps(range(0, peers - 1, 2)))
    parity = (lax.axis_index("req") % 2).astype(jnp.int32).reshape(1, 1)
    plan = jnp.concatenate([split_plan, parity], axis=1)
    (q,) = qkv_call(q_kernel, "queries", [(0, 0, local)], [(heads, AUG, count)], *inputs)
    acc, top = own_call(seg, q, kv)
    acc, top = near_call(plan, seg, q, acc, top, near)
    top, w_left, w_right = lax.optimization_barrier((top, w_left, w_right))
    w_top, w_end = beyond(w_left, w_right, "tp")
    pack = PACK * HD
    lows = list(range(0, local, pack))
    outs, sides = [], []
    for index in range(len(lows)):
        if outs:
            acc, outs[-1] = lax.optimization_barrier((acc, outs[-1]))
        outs.append(far_call(index * PACK, plan, seg, q, acc, top, far))
        if index == 1:
            outs[-1], w_top, w_end = lax.optimization_barrier((outs[-1], w_top, w_end))
        sides.append(beside(outs[-1], "tp"))
    w_far = [w_top, w_end]
    terms = [(part, w_out, low) for part, low in zip(outs, lows)]
    base = patches
    for index, (left, right) in enumerate(sides):
        if index:
            base, left, right = lax.optimization_barrier((base, left, right))
        opposite = beyond(left, right, "tp")
        terms += [(left, w_left, lows[index]), (right, w_right, lows[index])]
        base = gather_call(base, *zip(*terms))
        terms = [(opposite[0], w_far[index], 0), (opposite[1], w_far[index], opposite[0].shape[0])]
    within = jnp.arange(rows_out, dtype=jnp.int32) % lanes
    slot = (owner_dev * lanes + within).reshape(1, rows_out)
    send = project_call(
        slot, dest_row.reshape(1, rows_out), base, *zip(*terms), w_proj, peers * lanes
    )
    cols = send.shape[1]
    got = lax.all_to_all(send.reshape(peers, lanes, cols), "req", split_axis=0, concat_axis=0, tiled=True)
    return place_call(got.reshape(peers * lanes, cols), rows_out, w_proj.shape[1])


def solution(mesh):
    placed = (
        P("req", None),
        P("req"),
        P("req"),
        P("req", None),
        P("req"),
        P("req"),
        P(),
        P(),
        P(None, "tp", None),
        P("tp", None),
        P(None, "tp"),
    )
    return jax.shard_map(on_device, mesh=mesh, in_specs=placed, out_specs=P("req", "tp"), check_vma=False)
```

```python
import functools

import jax
import jax.numpy as jnp
import numpy as np
from jax import lax
from jax.experimental import pallas as pl
from jax.experimental.pallas import tpu as pltpu
from jax.sharding import PartitionSpec as P

HD = 88
QUARTER = HD // 4
SIDE_MAX = 32
AUG = 128
VAUG = 96
BIG = 1e30
TILE = 256
QB = 512
KB = 256
PACK = 2
F32 = jnp.float32
BF16 = jnp.bfloat16
NT = (((1,), (1,)), ((), ()))
NN = (((1,), (0,)), ((), ()))
TN = (((0,), (0,)), ((), ()))
LOG2E = 1.4426950408889634


def rope_table():
    freq = 10000.0 ** (-np.arange(QUARTER, dtype=np.float64) / QUARTER)
    chan = np.arange(HD)
    pos = np.arange(SIDE_MAX, dtype=np.float64)
    angle = freq[chan % QUARTER][:, None] * pos[None, :]
    sign = np.where(chan % (2 * QUARTER) < QUARTER, -1.0, 1.0)[:, None]
    in_row = (chan < 2 * QUARTER)[:, None]
    halves = []
    for part in (np.cos(angle), sign * np.sin(angle)):
        halves.append(np.concatenate([np.where(in_row, part, 0.0), np.where(in_row, 0.0, part)], axis=1))
    table = np.concatenate(halves, axis=0).astype(np.float32)
    terms = []
    for _ in range(3):
        term = table.astype(jnp.bfloat16)
        terms.append(term)
        table = table - term.astype(np.float32)
    return np.concatenate(terms, axis=1)


def seg_counts(seg):
    ids = lax.broadcasted_iota(jnp.int32, (16, seg.shape[1]), 0)
    below = jnp.sum((seg < ids).astype(F32), axis=1, keepdims=True)
    return below


def label_rows(label):
    ids = lax.broadcasted_iota(jnp.int32, (AUG - HD, label.shape[1]), 0)
    return (ids == jnp.where(label < 0, 16, label)).astype(F32)


def normalised(x_ref, gain_ref, bias_ref):
    x = x_ref[...].astype(F32)
    centred = x - jnp.mean(x, axis=1, keepdims=True)
    variance = jnp.mean(centred * centred, axis=1, keepdims=True)
    scaled = centred * lax.rsqrt(variance + 1e-6) * gain_ref[...].reshape(1, -1) + bias_ref[...].reshape(1, -1)
    return scaled.astype(BF16)


def rotations(plan_ref, table_ref, seg_ref, segt_ref, side_ref):
    below = seg_counts(seg_ref[...])
    seg = segt_ref[...]
    ids = lax.broadcasted_iota(jnp.int32, (16, TILE), 0)
    start = jnp.sum(jnp.where(ids == seg, below, 0.0), axis=0, keepdims=True).astype(jnp.int32)
    token = lax.broadcasted_iota(jnp.int32, (1, TILE), 1) + pl.program_id(0) * TILE
    offset = token - start + jnp.where(seg == 0, plan_ref[0, 0], 0)
    window = lax.shift_right_logical(offset, 2)
    corner = offset & 3
    half = lax.shift_right_logical(side_ref[...], 1)
    down = jnp.floor((window.astype(F32) + 0.5) / half.astype(F32)).astype(jnp.int32)
    grid_row = 2 * down + lax.shift_right_logical(corner, 1)
    grid_col = 2 * (window - down * half) + (corner & 1)
    pos = lax.broadcasted_iota(jnp.int32, (2 * SIDE_MAX, TILE), 0)
    hot = ((pos == grid_row) | (pos == grid_col + SIDE_MAX)).astype(F32).astype(BF16)
    hot = jnp.concatenate([hot, hot, hot], axis=0)
    angles = lax.dot_general(table_ref[...], hot, NN, preferred_element_type=F32)
    cosine, sine = angles[:HD], angles[HD:]
    first = lax.broadcasted_iota(jnp.int32, (HD, TILE), 0) % (2 * QUARTER) < QUARTER

    def rotated(value):
        partner = jnp.where(first, pltpu.roll(value, HD - QUARTER, 0), pltpu.roll(value, QUARTER, 0))
        return value * cosine + partner * sine

    return rotated


def qkv_kernel(plan_ref, table_ref, seg_ref, segt_ref, side_ref, x_ref, gain_ref, bias_ref, wk_ref, wv_ref, wq_ref, kv_ref, q_ref):
    normed = normalised(x_ref, gain_ref, bias_ref)
    rotated = rotations(plan_ref, table_ref, seg_ref, segt_ref, side_ref)
    keys = lax.dot_general(wk_ref[0], normed, NT, preferred_element_type=F32)
    values = lax.dot_general(wv_ref[0], normed, NT, preferred_element_type=F32)
    queries = lax.dot_general(wq_ref[0], normed, NT, preferred_element_type=F32)
    aug = lax.broadcasted_iota(jnp.int32, (AUG - HD, TILE), 0)
    barred = jnp.where(aug == jnp.broadcast_to(segt_ref[...], aug.shape), 0.0, jnp.where(aug <= 16, -BIG, 0.0))
    for h in range(q_ref.shape[0]):
        span = slice(h * HD, (h + 1) * HD)
        kv_ref[0, h] = rotated(keys[span]).astype(BF16)
        kv_ref[1, h] = values[span].astype(BF16)
        query = rotated(queries[span]) * (HD**-0.5 * LOG2E)
        q_ref[h] = jnp.concatenate([query, barred], axis=0).astype(BF16)


def qkv_call(kernel, name, rows, outs, patches, seg, sides, plan, gain, bias, w_qkv, table):
    count, width = patches.shape
    whole = lambda *shape: pl.BlockSpec(shape, lambda i: (0,) * len(shape))
    pick = lambda k, part, size: pl.BlockSpec((1, size, width), lambda i: (k, part, 0))
    flops = 2 * count * width * sum(size for _, _, size in rows)
    args = (plan, table, seg, seg, sides, patches, gain, bias) + (w_qkv,) * len(rows)
    return pl.pallas_call(
        kernel,
        grid=(count // TILE,),
        in_specs=[
            pl.BlockSpec(memory_space=pltpu.SMEM),
            whole(*table.shape),
            whole(1, count),
            pl.BlockSpec((1, TILE), lambda i: (0, i)),
            pl.BlockSpec((1, TILE), lambda i: (0, i)),
            pl.BlockSpec((TILE, width), lambda i: (i, 0)),
            whole(width),
            whole(width),
        ]
        + [pick(*row) for row in rows],
        out_specs=[
            pl.BlockSpec(shape[:-1] + (TILE,), lambda i, n=len(shape): (0,) * (n - 1) + (i,)) for shape in outs
        ],
        out_shape=[jax.ShapeDtypeStruct(shape, BF16) for shape in outs],
        compiler_params=pltpu.CompilerParams(vmem_limit_bytes=12 << 20),
        cost_estimate=pl.CostEstimate(flops=flops // 1, bytes_accessed=1 << 20, transcendentals=0),
        name=name,
    )(*[pltpu.with_memory_space_constraint(v, pltpu.HBM) for v in args])


def prepare_block(kv_ref, first, label, keys, values, base):
    rows = label_rows(label)
    extra = VAUG - HD
    ones = (lax.broadcasted_iota(jnp.int32, (extra, KB), 0) == 0).astype(F32)
    for h in range(keys.shape[0]):
        block = jnp.concatenate([kv_ref[0, first + h, :, pl.ds(base, KB)].astype(F32), rows], axis=0)
        keys[h, pl.ds(base, KB), :] = block.astype(BF16).T
        block = jnp.concatenate([kv_ref[1, first + h, :, pl.ds(base, KB)].astype(F32), ones], axis=0)
        values[h, :, pl.ds(base, KB)] = block.astype(BF16)


def attend(first, q_ref, keys, values, acc, top, q_base, k_base):
    heads = keys.shape[0]
    span = pl.ds(q_base, QB)
    old = [top[first + h : first + h + 1, span] for h in range(heads)]
    scores = [
        lax.dot_general(keys[h, pl.ds(k_base, KB), :], q_ref[first + h, :, span], NN, preferred_element_type=F32)
        for h in range(heads)
    ]
    new = [jnp.maximum(old[h], jnp.max(scores[h], axis=0, keepdims=True)) for h in range(heads)]
    weights = [jnp.exp2(scores[h] - new[h]).astype(BF16) for h in range(heads)]
    parts = [
        lax.dot_general(values[h, :, pl.ds(k_base, KB)], weights[h], NN, preferred_element_type=F32)
        for h in range(heads)
    ]
    sums = [acc[h, :, span] * jnp.exp2(old[h] - new[h]) + parts[h] for h in range(heads)]
    for h in range(heads):
        acc[h, :, span] = sums[h]
        top[first + h : first + h + 1, span] = new[h]


def own_kernel(sseg_ref, seg_ref, q_ref, kv_ref, acc_ref, top_ref, keys, values):
    count = seg_ref.shape[1]
    seg = seg_ref[...]
    for b in range(count // KB):
        prepare_block(kv_ref, 0, seg[:, b * KB : (b + 1) * KB], keys, values, b * KB)
    acc_ref[...] = jnp.zeros_like(acc_ref)
    top_ref[...] = jnp.full_like(top_ref, -BIG)

    def block(b, carry):
        q_base = pl.multiple_of(b * QB, QB)
        low = jnp.sum((seg < sseg_ref[0, q_base]).astype(jnp.int32))
        high = jnp.sum((seg <= sseg_ref[0, q_base + QB - 1]).astype(jnp.int32))

        def inner(k, c):
            attend(0, q_ref, keys, values, acc_ref, top_ref, q_base, pl.multiple_of(k * KB, KB))
            return c

        return lax.fori_loop(low // KB, (high + KB - 1) // KB, inner, carry)

    lax.fori_loop(0, count // QB, block, 0)


def neighbour(first, follows, plan_ref, sseg_ref, kv_ref, q_ref, keys, values, acc, top):
    count = q_ref.shape[2]
    last = sseg_ref[0, count - 1]
    begin = jnp.where(follows == 1, 0, count - plan_ref[0, 0])
    end = jnp.where(follows == 1, plan_ref[0, 1], count)
    image = jnp.where(follows == 1, last, 0)
    token = lax.broadcasted_iota(jnp.int32, (1, KB), 1)

    def block(k, carry):
        base = pl.multiple_of(k * KB, KB)
        label = jnp.where((token + base >= begin) & (token + base < end), image, -1)
        prepare_block(kv_ref, first, label, keys, values, base)

        def inner(b, c):
            q_base = pl.multiple_of(b * QB, QB)

            @pl.when(sseg_ref[0, q_base + follows * (QB - 1)] == image)
            def _():
                attend(first, q_ref, keys, values, acc, top, q_base, base)

            return c

        return lax.fori_loop(0, count // QB, inner, carry)

    lax.fori_loop(begin // KB, (end + KB - 1) // KB, block, 0)


def own_call(seg, q, kv):
    heads, _, count = q.shape
    vmem = pl.BlockSpec(memory_space=pltpu.VMEM)
    smem = pl.BlockSpec(memory_space=pltpu.SMEM)
    return pl.pallas_call(
        own_kernel,
        in_specs=[smem] + [vmem] * 3,
        out_specs=[vmem, vmem],
        out_shape=[
            jax.ShapeDtypeStruct((heads, VAUG, count), F32),
            jax.ShapeDtypeStruct((8, count), F32),
        ],
        scratch_shapes=[pltpu.VMEM((heads, count, AUG), BF16), pltpu.VMEM((heads, VAUG, count), BF16)],
        compiler_params=pltpu.CompilerParams(vmem_limit_bytes=10 << 20),
        cost_estimate=pl.CostEstimate(flops=64 << 28, bytes_accessed=1 << 20, transcendentals=0),
        name="own_keys",
    )(seg, seg, q, kv)


def near_kernel(plan_ref, sseg_ref, q_ref, acc_in, top_in, kv_ref, acc_ref, top_ref, keys, values):
    acc_ref[...] = acc_in[...]
    top_ref[...] = top_in[...]
    neighbour(0, 1 - plan_ref[0, 2], plan_ref, sseg_ref, kv_ref, q_ref, keys, values, acc_ref, top_ref)


def near_call(plan, seg, q, acc, top, kv):
    heads, _, count = q.shape
    vmem = pl.BlockSpec(memory_space=pltpu.VMEM)
    smem = pl.BlockSpec(memory_space=pltpu.SMEM)
    return pl.pallas_call(
        near_kernel,
        in_specs=[smem, smem, vmem, vmem, vmem, vmem],
        out_specs=[vmem, vmem],
        out_shape=[jax.ShapeDtypeStruct(acc.shape, F32), jax.ShapeDtypeStruct(top.shape, F32)],
        scratch_shapes=[pltpu.VMEM((heads, count, AUG), BF16), pltpu.VMEM((heads, VAUG, count), BF16)],
        compiler_params=pltpu.CompilerParams(vmem_limit_bytes=10 << 20),
        cost_estimate=pl.CostEstimate(flops=1 << 28, bytes_accessed=1 << 20, transcendentals=0),
        name="near_keys",
    )(plan, seg, q, acc, top, kv)


def far_kernel(first, plan_ref, sseg_ref, q_ref, acc_in, top_in, kv_ref, out_ref, acc, top, keys, values):
    heads = keys.shape[0]
    acc[...] = acc_in[first : first + heads]
    top[...] = top_in[...]
    neighbour(first, plan_ref[0, 2], plan_ref, sseg_ref, kv_ref, q_ref, keys, values, acc, top)
    for h in range(heads):
        out_ref[pl.ds(h * HD, HD), :] = (acc[h, :HD, :] * (1.0 / acc[h, HD : HD + 1, :])).astype(BF16)


def far_call(first, plan, seg, q, acc, top, kv):
    count = q.shape[2]
    vmem = pl.BlockSpec(memory_space=pltpu.VMEM)
    smem = pl.BlockSpec(memory_space=pltpu.SMEM)
    return pl.pallas_call(
        functools.partial(far_kernel, first),
        in_specs=[smem, smem, vmem, vmem, vmem, vmem],
        out_specs=vmem,
        out_shape=jax.ShapeDtypeStruct((PACK * HD, count), BF16),
        scratch_shapes=[
            pltpu.VMEM((PACK, VAUG, count), F32),
            pltpu.VMEM(top.shape, F32),
            pltpu.VMEM((PACK, count, AUG), BF16),
            pltpu.VMEM((PACK, VAUG, count), BF16),
        ],
        compiler_params=pltpu.CompilerParams(vmem_limit_bytes=10 << 20),
        cost_estimate=pl.CostEstimate(flops=12 << 28, bytes_accessed=1 << 20, transcendentals=0),
        name="far_keys",
    )(plan, seg, q, acc, top, kv)


def gather_kernel(parts, rows, base_ref, *refs):
    out_ref = refs[-1]
    for start in range(0, out_ref.shape[0], TILE):
        span = slice(start, start + TILE)
        total = base_ref[span].astype(F32)
        for h_ref, w_ref, row in zip(refs[:parts], refs[parts : 2 * parts], rows):
            w = w_ref[row : row + h_ref.shape[0]]
            total += lax.dot_general(h_ref[:, span], w, TN, preferred_element_type=F32)
        out_ref[span] = total


def gather_call(base, heads_parts, w_parts, rows):
    vmem = pl.BlockSpec(memory_space=pltpu.VMEM)
    parts = len(heads_parts)
    flops = 2 * base.shape[0] * base.shape[1] * sum(h.shape[0] for h in heads_parts)
    return pl.pallas_call(
        functools.partial(gather_kernel, parts, rows),
        in_specs=[vmem] * (1 + 2 * parts),
        out_specs=vmem,
        out_shape=jax.ShapeDtypeStruct(base.shape, F32),
        compiler_params=pltpu.CompilerParams(vmem_limit_bytes=12 << 20),
        cost_estimate=pl.CostEstimate(flops=flops // 8, bytes_accessed=1 << 16, transcendentals=0),
        name="output",
    )(base, *heads_parts, *w_parts)


def project_kernel(parts, starts, slot_ref, dest_ref, base_ref, *refs):
    proj, send_ref, mixed = refs[2 * parts :]
    count, width = base_ref.shape
    chunks = width // 128
    for start in range(0, count, TILE):
        span = slice(start, start + TILE)
        total = base_ref[span]
        for h_ref, w_ref, row in zip(refs[:parts], refs[parts : 2 * parts], starts):
            w = w_ref[row : row + h_ref.shape[0]]
            total += lax.dot_general(h_ref[:, span], w, TN, preferred_element_type=F32)
        for c in range(chunks):
            mixed[c, span, :] = total[:, c * 128 : (c + 1) * 128]
    rows = count // 4
    result = jnp.zeros((rows, proj.shape[1]), F32)
    for j in range(4):
        part = jnp.concatenate([mixed[c, pl.ds(j, rows, stride=4), :] for c in range(chunks)], axis=1).astype(BF16)
        result += lax.dot_general(part, proj[j * width : (j + 1) * width, :], NN, preferred_element_type=F32)
    slots = lax.broadcasted_iota(jnp.int32, (send_ref.shape[0], rows), 0)
    pick = (slots == slot_ref[...]).astype(F32)
    cols = proj.shape[1]
    send_ref[:, :cols] = lax.dot_general(
        pick.astype(BF16), result.astype(BF16), NN, preferred_element_type=F32
    ).astype(BF16)
    dest = jnp.sum(pick * dest_ref[...].astype(F32), axis=1, keepdims=True)
    send_ref[:, cols:] = jnp.broadcast_to(dest, (send_ref.shape[0], 128)).astype(BF16)


def project_call(slot, dest, base, heads_parts, w_parts, starts, w_proj, slots):
    vmem = pl.BlockSpec(memory_space=pltpu.VMEM)
    parts = len(heads_parts)
    count, width = base.shape
    cols = w_proj.shape[1]
    return pl.pallas_call(
        functools.partial(project_kernel, parts, starts),
        in_specs=[vmem] * (4 + 2 * parts),
        out_specs=vmem,
        out_shape=jax.ShapeDtypeStruct((slots, cols + 128), BF16),
        scratch_shapes=[pltpu.VMEM((width // 128, count, 128), F32)],
        compiler_params=pltpu.CompilerParams(vmem_limit_bytes=20 << 20),
        cost_estimate=pl.CostEstimate(flops=3 << 30, bytes_accessed=8 << 20, transcendentals=0),
        name="project",
    )(slot, dest, base, *heads_parts, *w_parts, w_proj)


def place_kernel(got_ref, out_ref):
    cols = out_ref.shape[1]
    dest = got_ref[:, cols:].astype(F32).astype(jnp.int32)
    dest = jnp.concatenate([dest] * (out_ref.shape[0] // 128), axis=1)
    rows = lax.broadcasted_iota(jnp.int32, dest.shape, 1)
    pick = (rows == dest).astype(F32).astype(BF16)
    out_ref[...] = lax.dot_general(pick, got_ref[:, :cols], TN, preferred_element_type=F32).astype(BF16)


def place_call(got, rows, cols):
    vmem = pl.BlockSpec(memory_space=pltpu.VMEM)
    return pl.pallas_call(
        place_kernel,
        in_specs=[vmem],
        out_specs=vmem,
        out_shape=jax.ShapeDtypeStruct((rows, cols), BF16),
        name="place",
    )(got)


def ring(axis, shift):
    size = lax.axis_size(axis)
    return [(i, (i + shift) % size) for i in range(size)]


def swaps(firsts):
    return [pair for i in firsts for pair in ((i, i + 1), (i + 1, i))]


def beside(block, axis):
    return lax.ppermute(block, axis, ring(axis, 1)), lax.ppermute(block, axis, ring(axis, -1))


def beyond(left, right, axis):
    half = -(-left.shape[0] // 32) * 16
    return lax.ppermute(left[:half], axis, ring(axis, 1)), lax.ppermute(right[half:], axis, ring(axis, -1))


def on_device(patches, segment_ids, grid_sides, split_plan, owner_dev, dest_row, ln_gain, ln_bias, w_qkv, w_out, w_proj):
    count, width = patches.shape
    local = w_qkv.shape[1]
    heads = local // HD
    rows_out = owner_dev.shape[0]
    peers = lax.axis_size("req")
    lanes = 2 * rows_out // peers
    seg = segment_ids.reshape(1, count)
    table = jnp.asarray(rope_table())
    w_left, w_right = beside(w_out, "tp")
    inputs = (patches, seg, grid_sides.reshape(1, count), split_plan, ln_gain, ln_bias, w_qkv, table)
    rows = [(1, 0, local), (2, 0, local), (0, 0, local)]
    kv, q = qkv_call(qkv_kernel, "qkv", rows, [(2, heads, HD, count), (heads, AUG, count)], *inputs)
    far = lax.ppermute(kv, "req", swaps(range(1, peers - 1, 2)))
    near = lax.ppermute(kv, "req", swaps(range(0, peers - 1, 2)))
    parity = (lax.axis_index("req") % 2).astype(jnp.int32).reshape(1, 1)
    plan = jnp.concatenate([split_plan, parity], axis=1)
    acc, top = own_call(seg, q, kv)
    acc, top = near_call(plan, seg, q, acc, top, near)
    top, w_left, w_right = lax.optimization_barrier((top, w_left, w_right))
    w_top, w_end = beyond(w_left, w_right, "tp")
    pack = PACK * HD
    lows = list(range(0, local, pack))
    outs, sides = [], []
    for index in range(len(lows)):
        if outs:
            acc, outs[-1] = lax.optimization_barrier((acc, outs[-1]))
        outs.append(far_call(index * PACK, plan, seg, q, acc, top, far))
        if index == 1:
            outs[-1], w_top, w_end = lax.optimization_barrier((outs[-1], w_top, w_end))
        sides.append(beside(outs[-1], "tp"))
    w_far = [w_top, w_end]
    terms = [(part, w_out, low) for part, low in zip(outs, lows)]
    base = patches
    for index, (left, right) in enumerate(sides):
        if index:
            base, left, right = lax.optimization_barrier((base, left, right))
        opposite = beyond(left, right, "tp")
        terms += [(left, w_left, lows[index]), (right, w_right, lows[index])]
        base = gather_call(base, *zip(*terms))
        terms = [(opposite[0], w_far[index], 0), (opposite[1], w_far[index], opposite[0].shape[0])]
    within = jnp.arange(rows_out, dtype=jnp.int32) % lanes
    slot = (owner_dev * lanes + within).reshape(1, rows_out)
    send = project_call(
        slot, dest_row.reshape(1, rows_out), base, *zip(*terms), w_proj, peers * lanes
    )
    cols = send.shape[1]
    got = lax.all_to_all(send.reshape(peers, lanes, cols), "req", split_axis=0, concat_axis=0, tiled=True)
    return place_call(got.reshape(peers * lanes, cols), rows_out, w_proj.shape[1])


def solution(mesh):
    placed = (
        P("req", None),
        P("req"),
        P("req"),
        P("req", None),
        P("req"),
        P("req"),
        P(),
        P(),
        P(None, "tp", None),
        P("tp", None),
        P(None, "tp"),
    )
    return jax.shard_map(on_device, mesh=mesh, in_specs=placed, out_specs=P("req", "tp"), check_vma=False)
```

```python
import functools

import jax
import jax.numpy as jnp
import numpy as np
from jax import lax
from jax.experimental import pallas as pl
from jax.experimental.pallas import tpu as pltpu
from jax.sharding import PartitionSpec as P

HD = 88
QUARTER = HD // 4
SIDE_MAX = 32
AUG = 128
VAUG = 96
BIG = 1e30
TILE = 256
QB = 512
KB = 256
PACK = 2
F32 = jnp.float32
BF16 = jnp.bfloat16
NT = (((1,), (1,)), ((), ()))
NN = (((1,), (0,)), ((), ()))
TN = (((0,), (0,)), ((), ()))
LOG2E = 1.4426950408889634


def rope_table():
    freq = 10000.0 ** (-np.arange(QUARTER, dtype=np.float64) / QUARTER)
    chan = np.arange(HD)
    pos = np.arange(SIDE_MAX, dtype=np.float64)
    angle = freq[chan % QUARTER][:, None] * pos[None, :]
    sign = np.where(chan % (2 * QUARTER) < QUARTER, -1.0, 1.0)[:, None]
    in_row = (chan < 2 * QUARTER)[:, None]
    halves = []
    for part in (np.cos(angle), sign * np.sin(angle)):
        halves.append(np.concatenate([np.where(in_row, part, 0.0), np.where(in_row, 0.0, part)], axis=1))
    table = np.concatenate(halves, axis=0).astype(np.float32)
    terms = []
    for _ in range(3):
        term = table.astype(jnp.bfloat16)
        terms.append(term)
        table = table - term.astype(np.float32)
    return np.concatenate(terms, axis=1)


def seg_counts(seg):
    ids = lax.broadcasted_iota(jnp.int32, (16, seg.shape[1]), 0)
    below = jnp.sum((seg < ids).astype(F32), axis=1, keepdims=True)
    return below


def label_rows(label):
    ids = lax.broadcasted_iota(jnp.int32, (AUG - HD, label.shape[1]), 0)
    return (ids == jnp.where(label < 0, 16, label)).astype(F32)


def normalised(x_ref, gain_ref, bias_ref):
    x = x_ref[...].astype(F32)
    centred = x - jnp.mean(x, axis=1, keepdims=True)
    variance = jnp.mean(centred * centred, axis=1, keepdims=True)
    scaled = centred * lax.rsqrt(variance + 1e-6) * gain_ref[...].reshape(1, -1) + bias_ref[...].reshape(1, -1)
    return scaled.astype(BF16)


def rotations(plan_ref, table_ref, seg_ref, segt_ref, side_ref):
    below = seg_counts(seg_ref[...])
    seg = segt_ref[...]
    ids = lax.broadcasted_iota(jnp.int32, (16, TILE), 0)
    start = jnp.sum(jnp.where(ids == seg, below, 0.0), axis=0, keepdims=True).astype(jnp.int32)
    token = lax.broadcasted_iota(jnp.int32, (1, TILE), 1) + pl.program_id(0) * TILE
    offset = token - start + jnp.where(seg == 0, plan_ref[0, 0], 0)
    window = lax.shift_right_logical(offset, 2)
    corner = offset & 3
    half = lax.shift_right_logical(side_ref[...], 1)
    down = jnp.floor((window.astype(F32) + 0.5) / half.astype(F32)).astype(jnp.int32)
    grid_row = 2 * down + lax.shift_right_logical(corner, 1)
    grid_col = 2 * (window - down * half) + (corner & 1)
    pos = lax.broadcasted_iota(jnp.int32, (2 * SIDE_MAX, TILE), 0)
    hot = ((pos == grid_row) | (pos == grid_col + SIDE_MAX)).astype(F32).astype(BF16)
    hot = jnp.concatenate([hot, hot, hot], axis=0)
    angles = lax.dot_general(table_ref[...], hot, NN, preferred_element_type=F32)
    cosine, sine = angles[:HD], angles[HD:]
    first = lax.broadcasted_iota(jnp.int32, (HD, TILE), 0) % (2 * QUARTER) < QUARTER

    def rotated(value):
        partner = jnp.where(first, pltpu.roll(value, HD - QUARTER, 0), pltpu.roll(value, QUARTER, 0))
        return value * cosine + partner * sine

    return rotated


def qkv_kernel(plan_ref, table_ref, seg_ref, segt_ref, side_ref, x_ref, gain_ref, bias_ref, wk_ref, wv_ref, wq_ref, kv_ref, q_ref):
    normed = normalised(x_ref, gain_ref, bias_ref)
    rotated = rotations(plan_ref, table_ref, seg_ref, segt_ref, side_ref)
    keys = lax.dot_general(wk_ref[0], normed, NT, preferred_element_type=F32)
    values = lax.dot_general(wv_ref[0], normed, NT, preferred_element_type=F32)
    queries = lax.dot_general(wq_ref[0], normed, NT, preferred_element_type=F32)
    aug = lax.broadcasted_iota(jnp.int32, (AUG - HD, TILE), 0)
    barred = jnp.where(aug == jnp.broadcast_to(segt_ref[...], aug.shape), 0.0, jnp.where(aug <= 16, -BIG, 0.0))
    for h in range(q_ref.shape[0]):
        span = slice(h * HD, (h + 1) * HD)
        kv_ref[0, h] = rotated(keys[span]).astype(BF16)
        kv_ref[1, h] = values[span].astype(BF16)
        query = rotated(queries[span]) * (HD**-0.5 * LOG2E)
        q_ref[h] = jnp.concatenate([query, barred], axis=0).astype(BF16)


def qkv_call(kernel, name, rows, outs, patches, seg, sides, plan, gain, bias, w_qkv, table):
    count, width = patches.shape
    whole = lambda *shape: pl.BlockSpec(shape, lambda i: (0,) * len(shape))
    pick = lambda k, part, size: pl.BlockSpec((1, size, width), lambda i: (k, part, 0))
    flops = 2 * count * width * sum(size for _, _, size in rows)
    args = (plan, table, seg, seg, sides, patches, gain, bias) + (w_qkv,) * len(rows)
    return pl.pallas_call(
        kernel,
        grid=(count // TILE,),
        in_specs=[
            pl.BlockSpec(memory_space=pltpu.SMEM),
            whole(*table.shape),
            whole(1, count),
            pl.BlockSpec((1, TILE), lambda i: (0, i)),
            pl.BlockSpec((1, TILE), lambda i: (0, i)),
            pl.BlockSpec((TILE, width), lambda i: (i, 0)),
            whole(width),
            whole(width),
        ]
        + [pick(*row) for row in rows],
        out_specs=[
            pl.BlockSpec(shape[:-1] + (TILE,), lambda i, n=len(shape): (0,) * (n - 1) + (i,)) for shape in outs
        ],
        out_shape=[pltpu.HBM(shape, BF16) for shape in outs],
        compiler_params=pltpu.CompilerParams(vmem_limit_bytes=12 << 20),
        cost_estimate=pl.CostEstimate(flops=flops // 1, bytes_accessed=1 << 20, transcendentals=0),
        name=name,
    )(*[pltpu.with_memory_space_constraint(v, pltpu.HBM) for v in args])


def prepare_block(kv_ref, first, label, keys, values, base):
    rows = label_rows(label)
    extra = VAUG - HD
    ones = (lax.broadcasted_iota(jnp.int32, (extra, KB), 0) == 0).astype(F32)
    for h in range(keys.shape[0]):
        block = jnp.concatenate([kv_ref[0, first + h, :, pl.ds(base, KB)].astype(F32), rows], axis=0)
        keys[h, pl.ds(base, KB), :] = block.astype(BF16).T
        block = jnp.concatenate([kv_ref[1, first + h, :, pl.ds(base, KB)].astype(F32), ones], axis=0)
        values[h, :, pl.ds(base, KB)] = block.astype(BF16)


def attend(first, q_ref, keys, values, acc, top, q_base, k_base):
    heads = keys.shape[0]
    span = pl.ds(q_base, QB)
    old = [top[first + h : first + h + 1, span] for h in range(heads)]
    scores = [
        lax.dot_general(keys[h, pl.ds(k_base, KB), :], q_ref[first + h, :, span], NN, preferred_element_type=F32)
        for h in range(heads)
    ]
    new = [jnp.maximum(old[h], jnp.max(scores[h], axis=0, keepdims=True)) for h in range(heads)]
    weights = [jnp.exp2(scores[h] - new[h]).astype(BF16) for h in range(heads)]
    parts = [
        lax.dot_general(values[h, :, pl.ds(k_base, KB)], weights[h], NN, preferred_element_type=F32)
        for h in range(heads)
    ]
    sums = [acc[h, :, span] * jnp.exp2(old[h] - new[h]) + parts[h] for h in range(heads)]
    for h in range(heads):
        acc[h, :, span] = sums[h]
        top[first + h : first + h + 1, span] = new[h]


def own_kernel(sseg_ref, seg_ref, q_ref, kv_ref, acc_ref, top_ref, keys, values):
    count = seg_ref.shape[1]
    seg = seg_ref[...]
    for b in range(count // KB):
        prepare_block(kv_ref, 0, seg[:, b * KB : (b + 1) * KB], keys, values, b * KB)
    acc_ref[...] = jnp.zeros_like(acc_ref)
    top_ref[...] = jnp.full_like(top_ref, -BIG)

    def block(b, carry):
        q_base = pl.multiple_of(b * QB, QB)
        low = jnp.sum((seg < sseg_ref[0, q_base]).astype(jnp.int32))
        high = jnp.sum((seg <= sseg_ref[0, q_base + QB - 1]).astype(jnp.int32))

        def inner(k, c):
            attend(0, q_ref, keys, values, acc_ref, top_ref, q_base, pl.multiple_of(k * KB, KB))
            return c

        return lax.fori_loop(low // KB, (high + KB - 1) // KB, inner, carry)

    lax.fori_loop(0, count // QB, block, 0)


def neighbour(first, follows, plan_ref, sseg_ref, kv_ref, q_ref, keys, values, acc, top):
    count = q_ref.shape[2]
    last = sseg_ref[0, count - 1]
    begin = jnp.where(follows == 1, 0, count - plan_ref[0, 0])
    end = jnp.where(follows == 1, plan_ref[0, 1], count)
    image = jnp.where(follows == 1, last, 0)
    token = lax.broadcasted_iota(jnp.int32, (1, KB), 1)

    def block(k, carry):
        base = pl.multiple_of(k * KB, KB)
        label = jnp.where((token + base >= begin) & (token + base < end), image, -1)
        prepare_block(kv_ref, first, label, keys, values, base)

        def inner(b, c):
            q_base = pl.multiple_of(b * QB, QB)

            @pl.when(sseg_ref[0, q_base + follows * (QB - 1)] == image)
            def _():
                attend(first, q_ref, keys, values, acc, top, q_base, base)

            return c

        return lax.fori_loop(0, count // QB, inner, carry)

    lax.fori_loop(begin // KB, (end + KB - 1) // KB, block, 0)


def own_call(seg, q, kv):
    heads, _, count = q.shape
    vmem = pl.BlockSpec(memory_space=pltpu.VMEM)
    smem = pl.BlockSpec(memory_space=pltpu.SMEM)
    return pl.pallas_call(
        own_kernel,
        in_specs=[smem] + [vmem] * 3,
        out_specs=[vmem, vmem],
        out_shape=[
            jax.ShapeDtypeStruct((heads, VAUG, count), F32),
            jax.ShapeDtypeStruct((8, count), F32),
        ],
        scratch_shapes=[pltpu.VMEM((heads, count, AUG), BF16), pltpu.VMEM((heads, VAUG, count), BF16)],
        compiler_params=pltpu.CompilerParams(vmem_limit_bytes=10 << 20),
        cost_estimate=pl.CostEstimate(flops=64 << 28, bytes_accessed=1 << 20, transcendentals=0),
        name="own_keys",
    )(seg, seg, q, kv)


def near_kernel(plan_ref, sseg_ref, q_ref, acc_in, top_in, kv_ref, acc_ref, top_ref, keys, values):
    acc_ref[...] = acc_in[...]
    top_ref[...] = top_in[...]
    neighbour(0, 1 - plan_ref[0, 2], plan_ref, sseg_ref, kv_ref, q_ref, keys, values, acc_ref, top_ref)


def near_call(plan, seg, q, acc, top, kv):
    heads, _, count = q.shape
    vmem = pl.BlockSpec(memory_space=pltpu.VMEM)
    smem = pl.BlockSpec(memory_space=pltpu.SMEM)
    return pl.pallas_call(
        near_kernel,
        in_specs=[smem, smem, vmem, vmem, vmem, vmem],
        out_specs=[vmem, vmem],
        out_shape=[jax.ShapeDtypeStruct(acc.shape, F32), jax.ShapeDtypeStruct(top.shape, F32)],
        scratch_shapes=[pltpu.VMEM((heads, count, AUG), BF16), pltpu.VMEM((heads, VAUG, count), BF16)],
        compiler_params=pltpu.CompilerParams(vmem_limit_bytes=10 << 20),
        cost_estimate=pl.CostEstimate(flops=1 << 28, bytes_accessed=1 << 20, transcendentals=0),
        name="near_keys",
    )(plan, seg, q, acc, top, kv)


def far_kernel(first, plan_ref, sseg_ref, q_ref, acc_in, top_in, kv_ref, out_ref, acc, top, keys, values):
    heads = keys.shape[0]
    acc[...] = acc_in[first : first + heads]
    top[...] = top_in[...]
    neighbour(first, plan_ref[0, 2], plan_ref, sseg_ref, kv_ref, q_ref, keys, values, acc, top)
    for h in range(heads):
        out_ref[pl.ds(h * HD, HD), :] = (acc[h, :HD, :] * (1.0 / acc[h, HD : HD + 1, :])).astype(BF16)


def far_call(first, plan, seg, q, acc, top, kv):
    count = q.shape[2]
    vmem = pl.BlockSpec(memory_space=pltpu.VMEM)
    smem = pl.BlockSpec(memory_space=pltpu.SMEM)
    return pl.pallas_call(
        functools.partial(far_kernel, first),
        in_specs=[smem, smem, vmem, vmem, vmem, vmem],
        out_specs=vmem,
        out_shape=jax.ShapeDtypeStruct((PACK * HD, count), BF16),
        scratch_shapes=[
            pltpu.VMEM((PACK, VAUG, count), F32),
            pltpu.VMEM(top.shape, F32),
            pltpu.VMEM((PACK, count, AUG), BF16),
            pltpu.VMEM((PACK, VAUG, count), BF16),
        ],
        compiler_params=pltpu.CompilerParams(vmem_limit_bytes=10 << 20),
        cost_estimate=pl.CostEstimate(flops=12 << 28, bytes_accessed=1 << 20, transcendentals=0),
        name="far_keys",
    )(plan, seg, q, acc, top, kv)


def gather_kernel(parts, rows, base_ref, *refs):
    out_ref = refs[-1]
    for start in range(0, out_ref.shape[0], TILE):
        span = slice(start, start + TILE)
        total = base_ref[span].astype(F32)
        for h_ref, w_ref, row in zip(refs[:parts], refs[parts : 2 * parts], rows):
            w = w_ref[row : row + h_ref.shape[0]]
            total += lax.dot_general(h_ref[:, span], w, TN, preferred_element_type=F32)
        out_ref[span] = total


def gather_call(base, heads_parts, w_parts, rows):
    vmem = pl.BlockSpec(memory_space=pltpu.VMEM)
    parts = len(heads_parts)
    flops = 2 * base.shape[0] * base.shape[1] * sum(h.shape[0] for h in heads_parts)
    return pl.pallas_call(
        functools.partial(gather_kernel, parts, rows),
        in_specs=[vmem] * (1 + 2 * parts),
        out_specs=vmem,
        out_shape=jax.ShapeDtypeStruct(base.shape, F32),
        compiler_params=pltpu.CompilerParams(vmem_limit_bytes=12 << 20),
        cost_estimate=pl.CostEstimate(flops=flops // 8, bytes_accessed=1 << 16, transcendentals=0),
        name="output",
    )(base, *heads_parts, *w_parts)


def project_kernel(parts, starts, slot_ref, dest_ref, base_ref, *refs):
    proj, send_ref, mixed = refs[2 * parts :]
    count, width = base_ref.shape
    chunks = width // 128
    for start in range(0, count, TILE):
        span = slice(start, start + TILE)
        total = base_ref[span]
        for h_ref, w_ref, row in zip(refs[:parts], refs[parts : 2 * parts], starts):
            w = w_ref[row : row + h_ref.shape[0]]
            total += lax.dot_general(h_ref[:, span], w, TN, preferred_element_type=F32)
        for c in range(chunks):
            mixed[c, span, :] = total[:, c * 128 : (c + 1) * 128]
    rows = count // 4
    result = jnp.zeros((rows, proj.shape[1]), F32)
    for j in range(4):
        part = jnp.concatenate([mixed[c, pl.ds(j, rows, stride=4), :] for c in range(chunks)], axis=1).astype(BF16)
        result += lax.dot_general(part, proj[j * width : (j + 1) * width, :], NN, preferred_element_type=F32)
    slots = lax.broadcasted_iota(jnp.int32, (send_ref.shape[0], rows), 0)
    pick = (slots == slot_ref[...]).astype(F32)
    cols = proj.shape[1]
    send_ref[:, :cols] = lax.dot_general(
        pick.astype(BF16), result.astype(BF16), NN, preferred_element_type=F32
    ).astype(BF16)
    dest = jnp.sum(pick * dest_ref[...].astype(F32), axis=1, keepdims=True)
    send_ref[:, cols:] = jnp.broadcast_to(dest, (send_ref.shape[0], 128)).astype(BF16)


def project_call(slot, dest, base, heads_parts, w_parts, starts, w_proj, slots):
    vmem = pl.BlockSpec(memory_space=pltpu.VMEM)
    parts = len(heads_parts)
    count, width = base.shape
    cols = w_proj.shape[1]
    return pl.pallas_call(
        functools.partial(project_kernel, parts, starts),
        in_specs=[vmem] * (4 + 2 * parts),
        out_specs=vmem,
        out_shape=jax.ShapeDtypeStruct((slots, cols + 128), BF16),
        scratch_shapes=[pltpu.VMEM((width // 128, count, 128), F32)],
        compiler_params=pltpu.CompilerParams(vmem_limit_bytes=20 << 20),
        cost_estimate=pl.CostEstimate(flops=3 << 30, bytes_accessed=8 << 20, transcendentals=0),
        name="project",
    )(slot, dest, base, *heads_parts, *w_parts, w_proj)


def place_kernel(got_ref, out_ref):
    cols = out_ref.shape[1]
    dest = got_ref[:, cols:].astype(F32).astype(jnp.int32)
    dest = jnp.concatenate([dest] * (out_ref.shape[0] // 128), axis=1)
    rows = lax.broadcasted_iota(jnp.int32, dest.shape, 1)
    pick = (rows == dest).astype(F32).astype(BF16)
    out_ref[...] = lax.dot_general(pick, got_ref[:, :cols], TN, preferred_element_type=F32).astype(BF16)


def place_call(got, rows, cols):
    vmem = pl.BlockSpec(memory_space=pltpu.VMEM)
    return pl.pallas_call(
        place_kernel,
        in_specs=[vmem],
        out_specs=vmem,
        out_shape=jax.ShapeDtypeStruct((rows, cols), BF16),
        name="place",
    )(got)


def ring(axis, shift):
    size = lax.axis_size(axis)
    return [(i, (i + shift) % size) for i in range(size)]


def swaps(firsts):
    return [pair for i in firsts for pair in ((i, i + 1), (i + 1, i))]


def beside(block, axis):
    return lax.ppermute(block, axis, ring(axis, 1)), lax.ppermute(block, axis, ring(axis, -1))


def beyond(left, right, axis):
    half = -(-left.shape[0] // 32) * 16
    return lax.ppermute(left[:half], axis, ring(axis, 1)), lax.ppermute(right[half:], axis, ring(axis, -1))


def on_device(patches, segment_ids, grid_sides, split_plan, owner_dev, dest_row, ln_gain, ln_bias, w_qkv, w_out, w_proj):
    count, width = patches.shape
    local = w_qkv.shape[1]
    heads = local // HD
    rows_out = owner_dev.shape[0]
    peers = lax.axis_size("req")
    lanes = 2 * rows_out // peers
    seg = segment_ids.reshape(1, count)
    table = jnp.asarray(rope_table())
    w_left, w_right = beside(w_out, "tp")
    inputs = (patches, seg, grid_sides.reshape(1, count), split_plan, ln_gain, ln_bias, w_qkv, table)
    rows = [(1, 0, local), (2, 0, local), (0, 0, local)]
    kv, q = qkv_call(qkv_kernel, "qkv", rows, [(2, heads, HD, count), (heads, AUG, count)], *inputs)
    far = lax.ppermute(kv, "req", swaps(range(1, peers - 1, 2)))
    near = lax.ppermute(kv, "req", swaps(range(0, peers - 1, 2)))
    parity = (lax.axis_index("req") % 2).astype(jnp.int32).reshape(1, 1)
    plan = jnp.concatenate([split_plan, parity], axis=1)
    acc, top = own_call(seg, q, kv)
    acc, top = near_call(plan, seg, q, acc, top, near)
    top, w_left, w_right = lax.optimization_barrier((top, w_left, w_right))
    w_top, w_end = beyond(w_left, w_right, "tp")
    pack = PACK * HD
    lows = list(range(0, local, pack))
    outs, sides = [], []
    for index in range(len(lows)):
        if outs:
            acc, outs[-1] = lax.optimization_barrier((acc, outs[-1]))
        outs.append(far_call(index * PACK, plan, seg, q, acc, top, far))
        if index == 1:
            outs[-1], w_top, w_end = lax.optimization_barrier((outs[-1], w_top, w_end))
        sides.append(beside(outs[-1], "tp"))
    w_far = [w_top, w_end]
    terms = [(part, w_out, low) for part, low in zip(outs, lows)]
    base = patches
    for index, (left, right) in enumerate(sides):
        if index:
            base, left, right = lax.optimization_barrier((base, left, right))
        opposite = beyond(left, right, "tp")
        terms += [(left, w_left, lows[index]), (right, w_right, lows[index])]
        base = gather_call(base, *zip(*terms))
        terms = [(opposite[0], w_far[index], 0), (opposite[1], w_far[index], opposite[0].shape[0])]
    within = jnp.arange(rows_out, dtype=jnp.int32) % lanes
    slot = (owner_dev * lanes + within).reshape(1, rows_out)
    send = project_call(
        slot, dest_row.reshape(1, rows_out), base, *zip(*terms), w_proj, peers * lanes
    )
    cols = send.shape[1]
    got = lax.all_to_all(send.reshape(peers, lanes, cols), "req", split_axis=0, concat_axis=0, tiled=True)
    return place_call(got.reshape(peers * lanes, cols), rows_out, w_proj.shape[1])


def solution(mesh):
    placed = (
        P("req", None),
        P("req"),
        P("req"),
        P("req", None),
        P("req"),
        P("req"),
        P(),
        P(),
        P(None, "tp", None),
        P("tp", None),
        P(None, "tp"),
    )
    return jax.shard_map(on_device, mesh=mesh, in_specs=placed, out_specs=P("req", "tp"), check_vma=False)
```
